32 devices in a mesh: dp: 8 (over z, x), mp: 4 (over y, core).
Axes of the slice: x: 2, y: 2, z: 4, core: 2. Of those that a mesh axis runs over, the one named last changes fastest.
Arguments:
- activations: bfloat16 [4096, 2560], P('dp'), may hold values from -6 to 6
- cotangent: bfloat16 [4096, 6912], P('dp', 'mp'), may hold values from -6 to 6
- frozen_weight: bfloat16 [2560, 6912], P(None, 'mp'), may hold values from -0.078125 to 0.078125
- skew_params: bfloat16 [10, 256, 256], replicated, may hold values from -0.125 to 0.125
- tile_order: int32 [20], replicated, may hold values from 0 to 19, each once
- block_owner: int32 [10], replicated, may hold values from 0 to 7, as said below
Outputs:
- input_grad: bfloat16 [4096, 2560], P('dp', 'mp')
- skew_grads: float32 [24, 256, 256], P('dp')
The draws below stay inside these ranges and needn't reach their ends.
Inputs may be any that keep to these rules, and one draw needn't show every extreme that they name: `tile_order`: a permutation of the 20 tiles. `block_owner`: no index of dp owns more than 3 blocks, and some index owns exactly 3; indices 0 and 8 - 1 own blocks in every draw.
All inputs are finite; a program needn't handle non-finite values.
Results may differ from the reference program's by a relative error of at most 0.001.
Values sent between devices are 32-bit elements; how exact they have to be, the bound alone decides.
A program may use at most 128 MiB of HBM per device.

```python
import math
import jax
import jax.numpy as jnp
from jax import lax

D = 2560
FF = 6912
BLOCK = 256
SLOTS = 3
TOKENS = 4096
TILES = 20
BLOCKS = 10
N_DP = 8


def draw_block_owner(key, part):
    first_key, second_key = jax.random.split(jax.random.fold_in(key, 17))
    groups = (jnp.arange(BLOCKS, dtype=jnp.int32) // SLOTS).astype(jnp.int32)
    shuffled = jax.random.permutation(first_key, BLOCKS)
    middle = (jax.random.permutation(second_key, N_DP - 2) + 1).astype(jnp.int32)
    heads = jnp.array([N_DP - 1, 0], dtype=jnp.int32)
    devices = jnp.concatenate([heads, middle.astype(jnp.int32)]).astype(jnp.int32)
    return devices[groups[shuffled]].astype(jnp.int32)


def block_levels(own_key, extent, shards, smallest, largest):
    loudness = 1.0
    for dim, blocks in shards:
        draws = jax.random.uniform(jax.random.fold_in(jax.random.fold_in(own_key, 6), dim), (blocks,), jnp.float32, smallest / len(shards), largest / len(shards))
        loudness = loudness * jnp.repeat(jnp.exp(draws), extent[dim] // blocks).reshape((-1,) + (1,) * (len(extent) - 1 - dim))
    return loudness


def scatter_about(key, shape, scale, limit, shards=(), kind=jnp.bfloat16):
    values = jax.random.normal(key, shape, jnp.float32) * scale
    if len(shards) > 0:
        values = block_levels(key, shape, shards, -0.22, 0.18) * values
    return jnp.clip(values, min=-limit, max=limit).astype(kind)


def setup_inputs(seed: int = 0) -> dict:
    keys = jax.random.split(jax.random.key(seed), 7)
    activations = scatter_about(keys[0], (TOKENS, D), 1.0, 6.0, ((0, 8),))
    cotangent = scatter_about(keys[1], (TOKENS, FF), 1.0, 6.0, ((0, 8), (1, 4)))
    frozen_weight = scatter_about(keys[2], (D, FF), FF ** -0.5, 0.078125, ((1, 4),))
    skew_params = scatter_about(keys[3], (BLOCKS, BLOCK, BLOCK), (0.14 * BLOCK ** -0.5), 0.125)
    tile_order = jax.random.permutation(keys[4], TILES).astype(jnp.int32)
    block_owner = draw_block_owner(jax.random.fold_in(keys[6], 71), 0)
    return dict(activations=activations, cotangent=cotangent, frozen_weight=frozen_weight, skew_params=skew_params, tile_order=tile_order, block_owner=block_owner)


highest = lax.Precision.HIGHEST

def product(first, second):
    return jnp.einsum('bij,bjk->bik', first, second, precision=highest)

def cayley_parts(params):
    plain = params.astype(jnp.float32)
    skew = plain - jnp.swapaxes(plain, 1, 2)
    square = product(skew, skew)
    cube = product(square, skew)
    identity = jnp.eye(skew.shape[1], dtype=jnp.float32)
    return (skew, identity[None] + 2.0 * skew + 2.0 * square + cube)

def to_blocks(matrix, order, tile_count, block_count):
    tiled = matrix.reshape(matrix.shape[0], tile_count, -1)
    return jnp.take(tiled, order, axis=1).reshape(matrix.shape[0], block_count, -1)

def from_blocks(blocked, order, tile_count):
    positions = jnp.arange(tile_count, dtype=jnp.int32)
    matches = (order[:, None] == positions[None, :]).astype(jnp.int32)
    inverse = lax.optimization_barrier(jnp.sum(positions[:, None] * matches, axis=0)).astype(jnp.int32)
    tiled = blocked.reshape(blocked.shape[0], tile_count, -1)
    return jnp.take(tiled, inverse, axis=1).reshape(blocked.shape[0], -1)

def adjoint(gram, skew):
    transposed = jnp.swapaxes(skew, 1, 2)
    left = product(gram, transposed)
    right = product(transposed, gram)
    total = 2.0 * gram + 2.0 * (left + right) + product(left, transposed) + product(transposed, left) + product(transposed, right)
    return total - jnp.swapaxes(total, 1, 2)

def reference(activations, cotangent, frozen_weight, skew_params, tile_order, block_owner):
    skew, rotation = cayley_parts(skew_params)
    feature_grad = jnp.dot(cotangent, frozen_weight.T, preferred_element_type=jnp.float32)
    grad_blocks = to_blocks(feature_grad, tile_order, TILES, BLOCKS)
    input_blocks = to_blocks(activations.astype(jnp.float32), tile_order, TILES, BLOCKS)
    rotated = jnp.einsum('tbj,bij->tbi', grad_blocks, rotation, precision=highest)
    input_grad = from_blocks(rotated, tile_order, TILES).astype(jnp.bfloat16)
    gram = jnp.einsum('tbi,tbj->bij', input_blocks, grad_blocks, precision=highest)
    block_grads = adjoint(gram, skew) * (1.0 / math.sqrt(TOKENS))
    numbers = jnp.arange(BLOCKS, dtype=jnp.int32)
    same_owner = block_owner[:, None] == block_owner[None, :]
    earlier = numbers[:, None] > numbers[None, :]
    ranking = lax.optimization_barrier(jnp.sum((same_owner & earlier).astype(jnp.int32), axis=1)).astype(jnp.int32)
    position = (block_owner * SLOTS + ranking).astype(jnp.int32)
    skew_grads = jnp.zeros((N_DP * SLOTS, BLOCK, BLOCK), jnp.float32).at[position].set(block_grads)
    return (input_grad, skew_grads)
```

```python
import functools
import math

import jax
import jax.numpy as jnp
from jax import lax
from jax.experimental import pallas as pl
from jax.experimental.pallas import tpu as pltpu
from jax.sharding import PartitionSpec as P

SLOTS = 3
LANES = 128
CHUNKS = 2
MESH = pl.DeviceIdType.MESH
F32 = jnp.float32
BF16 = jnp.bfloat16

NN = (((1,), (0,)), ((), ()))
NT = (((1,), (1,)), ((), ()))
TN = (((0,), (0,)), ((), ()))


def dot(a, b, dims=NN):
    return lax.dot_general(a, b, dims, preferred_element_type=F32)


def split(x):
    high = x.astype(BF16)
    return high, (x - high.astype(F32)).astype(BF16)


def dot_split(a, b):
    return dot(a[0], b[0]) + (dot(a[0], b[1]) + dot(a[1], b[0]))


def skew_of(params):
    plain = params.astype(F32)
    return plain - plain.T


def kernel(cfg, order_ref, owner_ref, act_hbm, cot_hbm, w_hbm, s_hbm, out_ref, grad_ref, *scratch):
    tokens, dim, block, blocks, tiles, n_dp, n_mp, own_gram = cfg
    (inv_ref, idx_ref, valid_ref, act_ref, cot_ref, cots, w_ref, s_ref, ls, acts, feat, outblk, part, eth, etl, recv1, send2, recv2, gram, grecv, gsum, arecv, hsum, zrecv, gpart, yrecv, gfull,
     slot_out, slot_in, slot_mate, s1, r1, s2, r2, gs, gr, xs, xr, ds, dr, ys, yr, ss, sr, ms, mr) = scratch
    half_mp = n_mp // 2
    rows = tokens // CHUNKS
    per = tiles // n_mp
    piece = block // 2 // n_dp
    dp = lax.axis_index("dp")
    mp = lax.axis_index("mp")
    side = lax.rem(mp, 2)
    group = mp // 2
    mate = group * 2 + (1 - side)

    load_s = pltpu.make_async_copy(s_hbm, s_ref, ls.at[blocks])
    load_cot = pltpu.make_async_copy(cot_hbm, cot_ref, ls.at[blocks + 1])
    load_act = pltpu.make_async_copy(act_hbm, act_ref, ls.at[blocks + 2])

    def load_w(n):
        at = pl.ds(pl.multiple_of(n * block, block), block)
        return pltpu.make_async_copy(w_hbm.at[:, at], w_ref.at[:, at], ls.at[n])

    load_s.start()
    load_cot.start()
    for n in range(blocks):
        load_w(n).start()
    load_act.start()

    def same_side(offset):
        return lax.rem(group + offset, half_mp)

    barrier = pltpu.get_barrier_semaphore()
    peers = []
    for o in range(half_mp):
        for k in range(2):
            if o or k:
                q = same_side(o)
                peers.append((dp, q * 2 + (side if k == 0 else 1 - side)))
    if own_gram:
        for o in range(1, n_dp):
            peers.append((lax.rem(dp + o, n_dp), mp))
    for peer in peers:
        pl.semaphore_signal(barrier, inc=1, device_id=peer, device_id_type=MESH)

    def invert(k, _):
        found = jnp.int32(0)
        for i in range(tiles):
            found = jnp.where(order_ref[i] == k, i, found)
        inv_ref[k] = found
        return 0

    lax.fori_loop(0, tiles, invert, 0)
    if own_gram:
        places = []
        for b in range(blocks):
            place = owner_ref[b] * SLOTS
            for e in range(b):
                place = place + jnp.where(owner_ref[e] == owner_ref[b], 1, 0)
            places.append(place)

        def locate(q, _):
            found = jnp.int32(0)
            count = jnp.float32(0.0)
            for b in range(blocks):
                found = jnp.where(places[b] == q, b, found)
                count = jnp.where(places[b] == q, 1.0, count)
            idx_ref[q] = found
            valid_ref[q] = count
            return 0

        lax.fori_loop(0, n_dp * SLOTS, locate, 0)

    def rotation(b, _):
        skew = skew_of(s_ref[b])
        pair = split(skew)
        square = dot_split(pair, pair)
        cube = dot_split(split(square), pair)
        high, low = split(2.0 * square - 2.0 * skew - cube)
        eth[b] = high
        etl[b] = low
        return 0

    load_s.wait()
    lax.fori_loop(0, blocks, rotation, 0)
    load_cot.wait()
    for i in range(tokens // LANES):
        cots[i * LANES:(i + 1) * LANES, :] = cot_ref[:, i * LANES:(i + 1) * LANES].T

    def features(j):
        def body(n, _):
            if j == 0:
                load_w(n).wait()
            f = dot(cots[j * rows:(j + 1) * rows, :], w_ref[:, pl.ds(pl.multiple_of(n * block, block), block)])
            feat[j * tiles + 2 * n] = f[:, :LANES]
            feat[j * tiles + 2 * n + 1] = f[:, LANES:]
            return 0
        lax.fori_loop(0, blocks, body, 0)

    def rotate(j):
        def body(b, _):
            t0 = order_ref[2 * b]
            t1 = order_ref[2 * b + 1]
            f = jnp.concatenate([feat[j * tiles + t0], feat[j * tiles + t1]], axis=1)
            high, low = split(f)
            out = f + (dot(high, eth[b]) + (dot(low, eth[b]) + dot(high, etl[b])))
            outblk[2 * b] = out[:, :LANES]
            outblk[2 * b + 1] = out[:, LANES:]
            return 0
        lax.fori_loop(0, blocks, body, 0)

    def grams():
        load_act.wait()
        for j in range(CHUNKS):
            for k in range(tiles):
                acts[j * tiles + k] = act_ref[j * rows:(j + 1) * rows, k * LANES:(k + 1) * LANES]

        def body(b, _):
            t0 = order_ref[2 * b]
            t1 = order_ref[2 * b + 1]
            g = 0.0
            for j in range(CHUNKS):
                f = jnp.concatenate([feat[j * tiles + t0], feat[j * tiles + t1]], axis=1)
                x = jnp.concatenate([acts[j * tiles + t0], acts[j * tiles + t1]], axis=1)
                high, low = split(f)
                g = g + (dot(x, high, TN) + dot(x, low, TN))
            if own_gram:
                for h in range(2):
                    for p in range(n_dp):
                        at = (h * n_dp + p) * piece
                        gram[h, p, b] = g[at:at + piece]
            else:
                grad_ref[b] = g
            return 0
        lax.fori_loop(0, blocks, body, 0)

    def permute(j):
        for q in range(n_mp):
            def body(i, _):
                part[j, q, i] = outblk[inv_ref[q * per + i]]
                return 0
            lax.fori_loop(0, per, body, 0)

    def first(j, o):
        q = same_side(o)
        return pltpu.make_async_remote_copy(
            src_ref=part.at[j, q * 2 + (1 - side)], dst_ref=recv1.at[j, q],
            send_sem=s1.at[j, o], recv_sem=r1.at[j, o],
            device_id=(dp, mate), device_id_type=MESH)

    def second(j, o):
        q = same_side(o)
        return pltpu.make_async_remote_copy(
            src_ref=send2.at[j, o - 1], dst_ref=recv2.at[j, o - 1],
            send_sem=s2.at[j, o - 1], recv_sem=r2.at[j, o - 1],
            device_id=(dp, q * 2 + side), device_id_type=MESH)

    order1 = list(range(1, half_mp)) + [0]

    def start_first(j):
        for o in order1:
            first(j, o).start()

    def start_second(j):
        for o in range(1, half_mp):
            first(j, o).wait_recv()
            q = same_side(o)
            for i in range(per):
                send2[j, o - 1, i] = part[j, q * 2 + side, i] + recv1[j, q, i]
            second(j, o).start()

    def finish(j):
        first(j, 0).wait_recv()
        for o in range(1, half_mp):
            second(j, o).wait_recv()
        for i in range(per):
            total = part[j, mp, i] + recv1[j, group, i]
            for o in range(1, half_mp):
                total = total + recv2[j, o - 1, i]
            out_ref[j * rows:(j + 1) * rows, i * LANES:(i + 1) * LANES] = total.astype(out_ref.dtype)

    features(0)
    rotate(0)
    permute(0)
    pl.semaphore_wait(barrier, len(peers))
    start_first(0)
    for j in range(1, CHUNKS):
        features(j)
        start_second(j - 1)
        if j == CHUNKS - 1:
            grams()
            if own_gram:
                swap = pltpu.make_async_remote_copy(
                    src_ref=gram.at[1 - side], dst_ref=grecv, send_sem=gs.at[0], recv_sem=gr.at[0],
                    device_id=(dp, mate), device_id_type=MESH)
                swap.start()
        rotate(j)
        permute(j)
        start_first(j)
    last = CHUNKS - 1

    start_second(last)
    if own_gram:
        swap.wait_recv()

        parity = lax.rem(dp, 2)
        line = dp // 2
        n_line = n_dp // 2
        parts = gsum.shape[1]
        some = blocks // parts

        def cross(g):
            return pltpu.make_async_remote_copy(
                src_ref=gsum.at[1 - parity, g], dst_ref=arecv.at[g], send_sem=xs.at[g], recv_sem=xr.at[g],
                device_id=(dp + 1 - 2 * parity, mp), device_id_type=MESH)

        def along(g, o):
            to = lax.rem(line + o, n_line)
            return pltpu.make_async_remote_copy(
                src_ref=hsum.at[g, to], dst_ref=zrecv.at[g, o - 1],
                send_sem=ds.at[g, o - 1], recv_sem=dr.at[g, o - 1],
                device_id=(to * 2 + parity, mp), device_id_type=MESH)

        for g in range(parts):
            def add_half(q, _):
                own = pl.ds(g * some, some)
                for t in range(2):
                    gsum[t, g, q] = gram[side, 2 * q + t, own] + grecv[2 * q + t, own]
                return 0
            lax.fori_loop(0, n_line, add_half, 0)
            cross(g).start()
        for g in range(parts):
            cross(g).wait_recv()

            def add_cross(q, _):
                hsum[g, q] = gsum[parity, g, q] + arecv[g, q]
                return 0
            lax.fori_loop(0, n_line, add_cross, 0)
            for o in range(1, n_line):
                along(g, o).start()
        for j in range(last):
            finish(j)

        def turn(s, _):
            eth[s], etl[s] = split(-skew_of(s_ref[idx_ref[dp * SLOTS + s]]))
            return 0
        lax.fori_loop(0, SLOTS, turn, 0)
        for g in range(parts):
            for o in range(1, n_line):
                along(g, o).wait_recv()
            total = hsum[g, line]
            for o in range(1, n_line):
                total = total + zrecv[g, o - 1]
            gpart[g * some:(g + 1) * some] = total

        def across(o):
            return pltpu.make_async_remote_copy(
                src_ref=gpart, dst_ref=yrecv.at[o - 1],
                send_sem=ys.at[o - 1], recv_sem=yr.at[o - 1],
                device_id=(dp, same_side(o) * 2 + side), device_id_type=MESH)

        for o in range(1, half_mp):
            across(o).start()
        for o in range(1, half_mp):
            across(o).wait_recv()

        def add_y(b, _):
            total = gpart[b]
            for o in range(1, half_mp):
                total = total + yrecv[o - 1, b]
            gfull[b] = total
            return 0
        lax.fori_loop(0, blocks, add_y, 0)

        for d in range(n_dp):
            for s in range(SLOTS):
                slot_out[d, s] = gfull[idx_ref[d * SLOTS + s]] * valid_ref[d * SLOTS + s]

        def deliver(o):
            to = lax.rem(dp + o, n_dp)
            return pltpu.make_async_remote_copy(
                src_ref=slot_out.at[to], dst_ref=slot_in.at[dp],
                send_sem=ss.at[o], recv_sem=sr.at[o],
                device_id=(to, mp), device_id_type=MESH)

        for o in range(1, n_dp):
            deliver(o).start()
        mine = pltpu.make_async_copy(slot_out.at[dp], slot_in.at[dp], ss.at[0])
        mine.start()
        mine.wait()
        finish(last)
        for o in range(1, n_dp):
            deliver(o).wait_recv()
        share = pltpu.make_async_remote_copy(
            src_ref=slot_in, dst_ref=slot_mate, send_sem=ms.at[0], recv_sem=mr.at[0],
            device_id=(dp, mate), device_id_type=MESH)
        share.start()
        share.wait_recv()
        upper = jnp.where(side == 0, 0.0, 1.0)

        def adjoint(s, _):
            own = jnp.concatenate([slot_in[p, s] for p in range(n_dp)], axis=0)
            other = jnp.concatenate([slot_mate[p, s] for p in range(n_dp)], axis=0)
            g = jnp.concatenate([own * (1.0 - upper) + other * upper, own * upper + other * (1.0 - upper)], axis=0)
            qt = (eth[s], etl[s])
            gp = split(g)
            left = dot_split(gp, qt)
            both = left + dot_split(qt, gp)
            total = 2.0 * g + 2.0 * both + dot_split(split(left), qt) + dot_split(qt, split(both))
            grad_ref[s] = (total - total.T) * (1.0 / math.sqrt(tokens * n_dp))
            return 0
        lax.fori_loop(0, SLOTS, adjoint, 0)
        swap.wait_send()
        for g in range(parts):
            cross(g).wait_send()
            for o in range(1, n_line):
                along(g, o).wait_send()
        for o in range(1, half_mp):
            across(o).wait_send()
        share.wait_send()
        for o in range(1, n_dp):
            deliver(o).wait_send()
    else:
        for j in range(CHUNKS):
            finish(j)
    for j in range(CHUNKS):
        for o in range(half_mp):
            first(j, o).wait_send()
        for o in range(1, half_mp):
            second(j, o).wait_send()


def publish(first, second):
    def body(a_ref, b_ref, oa_ref, ob_ref, sems):
        one = pltpu.make_async_copy(a_ref, oa_ref, sems.at[0])
        two = pltpu.make_async_copy(b_ref, ob_ref, sems.at[1])
        one.start()
        two.start()
        one.wait()
        two.wait()

    vmem = pl.BlockSpec(memory_space=pltpu.VMEM)
    hbm = pl.BlockSpec(memory_space=pl.ANY)
    return pl.pallas_call(
        body,
        out_shape=(jax.ShapeDtypeStruct(first.shape, first.dtype), jax.ShapeDtypeStruct(second.shape, second.dtype)),
        in_specs=[vmem, vmem],
        out_specs=(hbm, hbm),
        scratch_shapes=[pltpu.SemaphoreType.DMA((2,))],
        compiler_params=pltpu.CompilerParams(vmem_limit_bytes=2 * 1024 * 1024),
    )(first, second)


def local(n_dp, n_mp, activations, cotangent, frozen_weight, skew_params, tile_order, block_owner):
    tokens, dim = activations.shape
    hidden = cotangent.shape[1]
    blocks, block, _ = skew_params.shape
    tiles = tile_order.shape[0]
    piece = block // 2 // n_dp
    own_gram = piece * n_dp * 2 == block and piece % 8 == 0 and n_dp % 2 == 0
    keep = piece if own_gram else 8
    ring = n_dp if own_gram else 2
    width = blocks if own_gram else 1
    parts = next(k for k in (5, 2, 1) if width % k == 0)
    half_mp = n_mp // 2
    rows = tokens // CHUNKS
    per = tiles // n_mp

    cfg = (tokens, dim, block, blocks, tiles, n_dp, n_mp, own_gram)
    smem = pl.BlockSpec(memory_space=pltpu.SMEM)
    vmem = pl.BlockSpec(memory_space=pltpu.VMEM)
    dma = pltpu.SemaphoreType.DMA
    span = max(half_mp - 1, 1)
    grad_shape = (SLOTS if own_gram else blocks, block, block)
    input_grad, grads = pl.pallas_call(
        functools.partial(kernel, cfg),
        out_shape=(jax.ShapeDtypeStruct((tokens, dim // n_mp), BF16), jax.ShapeDtypeStruct(grad_shape, F32)),
        in_specs=[smem] * 2 + [pl.BlockSpec(memory_space=pl.ANY)] * 4,
        out_specs=(vmem, vmem),
        scratch_shapes=[
            pltpu.SMEM((tiles,), jnp.int32),
            pltpu.SMEM((n_dp * SLOTS,), jnp.int32),
            pltpu.SMEM((n_dp * SLOTS,), F32),
            pltpu.VMEM((tokens, dim), BF16),
            pltpu.VMEM((hidden, tokens), BF16),
            pltpu.VMEM((tokens, hidden), BF16),
            pltpu.VMEM((hidden, dim), BF16),
            pltpu.VMEM((blocks, block, block), BF16),
            dma((blocks + 3,)),
            pltpu.VMEM((CHUNKS * tiles, rows, LANES), BF16),
            pltpu.VMEM((CHUNKS * tiles, rows, LANES), F32),
            pltpu.VMEM((tiles, rows, LANES), F32),
            pltpu.VMEM((CHUNKS, n_mp, per, rows, LANES), F32),
            pltpu.VMEM((blocks, block, block), BF16),
            pltpu.VMEM((blocks, block, block), BF16),
            pltpu.VMEM((CHUNKS, half_mp, per, rows, LANES), F32),
            pltpu.VMEM((CHUNKS, span, per, rows, LANES), F32),
            pltpu.VMEM((CHUNKS, span, per, rows, LANES), F32),
            pltpu.VMEM((2, ring, width, keep, block), F32),
            pltpu.VMEM((ring, width, keep, block), F32),
            pltpu.VMEM((2, parts, ring // 2, width // parts, keep, block), F32),
            pltpu.VMEM((parts, ring // 2, width // parts, keep, block), F32),
            pltpu.VMEM((parts, ring // 2, width // parts, keep, block), F32),
            pltpu.VMEM((parts, max(ring // 2 - 1, 1), width // parts, keep, block), F32),
            pltpu.VMEM((width, keep, block), F32),
            pltpu.VMEM((span, width, keep, block), F32),
            pltpu.VMEM((width, keep, block), F32),
            pltpu.VMEM((ring, SLOTS, keep, block), F32),
            pltpu.VMEM((ring, SLOTS, keep, block), F32),
            pltpu.VMEM((ring, SLOTS, keep, block), F32),
            dma((CHUNKS, half_mp)), dma((CHUNKS, half_mp)),
            dma((CHUNKS, span)), dma((CHUNKS, span)),
            dma((1,)), dma((1,)),
            dma((parts,)), dma((parts,)),
            dma((parts, max(ring // 2 - 1, 1))), dma((parts, max(ring // 2 - 1, 1))),
            dma((span,)), dma((span,)),
            dma((ring,)), dma((ring,)),
            dma((1,)), dma((1,)),
        ],
        compiler_params=pltpu.CompilerParams(
            collective_id=0, has_side_effects=True, vmem_limit_bytes=52 * 1024 * 1024),
    )(tile_order, block_owner, activations, cotangent.T, frozen_weight.T, skew_params)
    if own_gram:
        return publish(input_grad, grads)
    numbers = jnp.arange(blocks, dtype=jnp.int32)
    same = block_owner[:, None] == block_owner[None, :]
    rank = jnp.sum((same & (numbers[:, None] > numbers[None, :])).astype(jnp.int32), axis=1)
    place = block_owner * SLOTS + rank
    chosen = place[None, :] == jnp.arange(n_dp * SLOTS, dtype=jnp.int32)[:, None]
    index = jnp.sum(jnp.where(chosen, numbers[None, :], 0), axis=1)
    valid = jnp.sum(chosen.astype(F32), axis=1)
    gram = lax.psum(grads, ("dp", "mp"))
    at = lax.axis_index("dp") * SLOTS
    mine = lax.dynamic_slice(index, (at,), (SLOTS,))
    used = lax.dynamic_slice(valid, (at,), (SLOTS,))
    g = jnp.take(gram, mine, axis=0) * used[:, None, None]
    plain = jnp.take(skew_params, mine, axis=0).astype(F32)
    qt = jnp.swapaxes(plain, 1, 2) - plain
    mul = functools.partial(jnp.einsum, "bij,bjk->bik", precision=lax.Precision.HIGHEST)
    left = mul(g, qt)
    both = left + mul(qt, g)
    total = 2.0 * g + 2.0 * both + mul(left, qt) + mul(qt, both)
    return input_grad, (total - jnp.swapaxes(total, 1, 2)) * (1.0 / math.sqrt(tokens * n_dp))


def solution(mesh):
    placed = (P("dp", None), P("dp", "mp"), P(None, "mp"), P(), P(), P())
    return jax.shard_map(
        functools.partial(local, mesh.shape["dp"], mesh.shape["mp"]),
        mesh=mesh,
        in_specs=placed,
        out_specs=(P("dp", "mp"), P("dp", None, None)),
        check_vma=False,
    )
```

```python
import functools
import math

import jax
import jax.numpy as jnp
from jax import lax
from jax.experimental import pallas as pl
from jax.experimental.pallas import tpu as pltpu
from jax.sharding import PartitionSpec as P

SLOTS = 3
LANES = 128
MESH = pl.DeviceIdType.MESH
F32 = jnp.float32
BF16 = jnp.bfloat16

NN = (((1,), (0,)), ((), ()))
TN = (((0,), (0,)), ((), ()))


def dot(a, b, dims=NN):
    return lax.dot_general(a, b, dims, preferred_element_type=F32)


def split(x):
    high = x.astype(BF16)
    return high, (x - high.astype(F32)).astype(BF16)


def dot_split(a, b):
    return dot(a[0], b[0]) + (dot(a[0], b[1]) + dot(a[1], b[0]))


def skew_of(params):
    plain = params.astype(F32)
    return plain - plain.T


def cuts(tokens):
    first = tokens * 3 // 8 // 16 * 16
    return ((0, first), (first, tokens)) if first else ((0, tokens),)


def kernel(cfg, order_ref, owner_ref, act_hbm, cot_hbm, w_hbm, s_hbm, out_ref, grad_ref, *scratch):
    tokens, dim, block, blocks, tiles, n_dp, n_mp, own_gram = cfg
    (inv_ref, idx_ref, valid_ref, cot_ref, cots, w_ref, s_ref, acts, feat, outblk, part, recv1, send2, recv2,
     sh, sl, eth, etl, esend, erecv, gsend, gown, grecv, pk, arecv, hsum, zrecv, gp, ax, gfull, slot_out, slot_in,
     lw, la, lo, es, er, s1, r1, s2, r2, gs, gr, xs, xr, ds, dr, ys, yr, ss, sr, ms, mr) = scratch
    half_mp = n_mp // 2
    half = blocks // 2
    per = tiles // n_mp
    chunks = cuts(tokens)
    last = len(chunks) - 1
    dp = lax.axis_index("dp")
    mp = lax.axis_index("mp")
    side = lax.rem(mp, 2)
    group = mp // 2
    mate = group * 2 + (1 - side)

    load_s = pltpu.make_async_copy(s_hbm, s_ref, lo.at[0])
    load_cot = pltpu.make_async_copy(cot_hbm, cot_ref, lo.at[1])

    def load_w(n):
        at = pl.ds(pl.multiple_of(n * block, block), block)
        return pltpu.make_async_copy(w_hbm.at[:, at], w_ref.at[:, at], lw.at[n])

    def load_act(k):
        return pltpu.make_async_copy(act_hbm.at[:, k * LANES:(k + 1) * LANES], acts.at[k], la.at[k])

    load_s.start()
    load_cot.start()
    for n in range(blocks):
        load_w(n).start()
    for k in range(tiles):
        load_act(k).start()

    def same_side(offset):
        return lax.rem(group + offset, half_mp)

    barrier = pltpu.get_barrier_semaphore()
    peers = []
    for o in range(half_mp):
        for k in range(2):
            if o or k:
                peers.append((dp, same_side(o) * 2 + (side if k == 0 else 1 - side)))
    if own_gram:
        for o in range(1, n_dp):
            peers.append((lax.rem(dp + o, n_dp), mp))
        for k in range(2):
            peers.append((dp + 1 - 2 * lax.rem(dp, 2), (1 - group) * 2 + (side if k == 0 else 1 - side)))
    for peer in peers:
        pl.semaphore_signal(barrier, inc=1, device_id=peer, device_id_type=MESH)

    def invert(k, _):
        found = jnp.int32(0)
        for i in range(tiles):
            found = jnp.where(order_ref[i] == k, i, found)
        inv_ref[k] = found
        return 0

    lax.fori_loop(0, tiles, invert, 0)

    def tell(i):
        return pltpu.make_async_remote_copy(
            src_ref=esend.at[i], dst_ref=erecv.at[i], send_sem=es.at[i], recv_sem=er.at[i],
            device_id=(dp, mate), device_id_type=MESH)

    load_s.wait()
    for i in range(half):
        b = side * half + i
        skew = skew_of(s_ref[b])
        pair = split(skew)
        sh[i], sl[i] = pair
        square = dot_split(pair, pair)
        cube = dot_split(split(square), pair)
        turned = 2.0 * square - 2.0 * skew - cube
        esend[i] = turned
        eth[b], etl[b] = split(turned)
    pl.semaphore_wait(barrier, len(peers))
    for i in range(half):
        tell(i).start()

    load_cot.wait()
    for i in range(tokens // LANES):
        cots[i * LANES:(i + 1) * LANES, :] = cot_ref[:, i * LANES:(i + 1) * LANES].T

    def feature(n, at):
        a, z = at
        f = dot(cots[a:z, :], w_ref[:, pl.ds(pl.multiple_of(n * block, block), block)])
        feat[2 * n, a:z] = f[:, :LANES]
        feat[2 * n + 1, a:z] = f[:, LANES:]

    def first_features(k, _):
        for u in range(2):
            load_w(2 * k + u).wait()
        for u in range(2):
            feature(2 * k + u, chunks[0])
        return 0

    def rotate(j):
        a, z = chunks[j]

        def body(k, _):
            for u in range(half):
                b = k * half + u
                f = jnp.concatenate([feat[order_ref[2 * b], a:z], feat[order_ref[2 * b + 1], a:z]], axis=1)
                high, low = split(f)
                out = f + (dot(high, eth[b]) + (dot(low, eth[b]) + dot(high, etl[b])))
                outblk[j][2 * b] = out[:, :LANES]
                outblk[j][2 * b + 1] = out[:, LANES:]
            return 0
        lax.fori_loop(0, 2, body, 0)

    def first(j, o, i):
        q = same_side(o)
        return pltpu.make_async_remote_copy(
            src_ref=part[j].at[q, i], dst_ref=recv1[j].at[q, i],
            send_sem=s1.at[j, o, i], recv_sem=r1.at[j, o, i],
            device_id=(dp, mate), device_id_type=MESH)

    def second(j, o, i):
        return pltpu.make_async_remote_copy(
            src_ref=send2[j].at[o - 1, i], dst_ref=recv2[j].at[o - 1, i],
            send_sem=s2.at[j, o - 1, i], recv_sem=r2.at[j, o - 1, i],
            device_id=(dp, same_side(o) * 2 + side), device_id_type=MESH)

    def start_first(j):
        for o in list(range(1, half_mp)) + [0]:
            q = same_side(o)
            for i in range(per):
                part[j][q, i] = outblk[j][inv_ref[(q * 2 + (1 - side)) * per + i]]
                first(j, o, i).start()

    def start_second(j):
        for o in range(1, half_mp):
            q = same_side(o)
            for i in range(per):
                first(j, o, i).wait_recv()
                send2[j][o - 1, i] = outblk[j][inv_ref[(q * 2 + side) * per + i]] + recv1[j][q, i]
                second(j, o, i).start()

    def finish(j):
        a, z = chunks[j]
        for i in range(per):
            first(j, 0, i).wait_recv()
            total = outblk[j][inv_ref[mp * per + i]] + recv1[j][group, i]
            for o in range(1, half_mp):
                second(j, o, i).wait_recv()
                total = total + recv2[j][o - 1, i]
            out_ref[a:z, i * LANES:(i + 1) * LANES] = total.astype(out_ref.dtype)

    def gram_of(b):
        t0 = order_ref[2 * b]
        t1 = order_ref[2 * b + 1]
        high, low = split(jnp.concatenate([feat[t0], feat[t1]], axis=1))
        x = jnp.concatenate([acts[t0], acts[t1]], axis=1)
        return dot(x, high, TN) + dot(x, low, TN)

    def swap(i):
        return pltpu.make_async_remote_copy(
            src_ref=gsend.at[i], dst_ref=grecv.at[i], send_sem=gs.at[i], recv_sem=gr.at[i],
            device_id=(dp, mate), device_id_type=MESH)

    lax.fori_loop(0, blocks // 2, first_features, 0)
    for i in range(half):
        tell(i).wait_recv()
        b = (1 - side) * half + i
        eth[b], etl[b] = split(erecv[i])
    rotate(0)
    start_first(0)
    for j in range(1, last + 1):
        for n in range(half):
            feature(n, chunks[j])
        start_second(j - 1)
        for n in range(half, blocks):
            feature(n, chunks[j])
    for k in range(tiles):
        load_act(k).wait()

    if own_gram:
        parity = lax.rem(dp, 2)
        line = dp // 2
        n_line = n_dp // 2
        piece = block // 2 // n_dp
        mine = lax.rem(parity + group, 2)
        across = dp + 1 - 2 * parity

        def cross(i):
            return pltpu.make_async_remote_copy(
                src_ref=pk.at[i, 1 - mine], dst_ref=arecv.at[i], send_sem=xs.at[i], recv_sem=xr.at[i],
                device_id=(across, mp), device_id_type=MESH)

        def along(i, o):
            to = lax.rem(line + o, n_line)
            return pltpu.make_async_remote_copy(
                src_ref=hsum.at[i, to], dst_ref=zrecv.at[i, o - 1],
                send_sem=ds.at[i, o - 1], recv_sem=dr.at[i, o - 1],
                device_id=(to * 2 + parity, mp), device_id_type=MESH)

        def trade(k):
            column = side if k == 1 else 1 - side
            to = (dp, mate) if k == 0 else (across, (1 - group) * 2 + column)
            return pltpu.make_async_remote_copy(
                src_ref=gp.at[column], dst_ref=ax.at[k], send_sem=ys.at[k], recv_sem=yr.at[k],
                device_id=to, device_id_type=MESH)

        def deliver(o):
            to = lax.rem(dp + o, n_dp)
            return pltpu.make_async_remote_copy(
                src_ref=slot_out.at[to], dst_ref=slot_in.at[side, dp],
                send_sem=ss.at[o], recv_sem=sr.at[o],
                device_id=(to, mp), device_id_type=MESH)

        share = pltpu.make_async_remote_copy(
            src_ref=slot_in.at[side], dst_ref=slot_in.at[side], send_sem=ms.at[0], recv_sem=mr.at[0],
            device_id=(dp, mate), device_id_type=MESH)

        row = lax.broadcasted_iota(jnp.int32, (LANES, LANES), 0)
        column = lax.broadcasted_iota(jnp.int32, (LANES, LANES), 1)

        for i in range(half):
            gsend[i] = gram_of((1 - side) * half + i)
            swap(i).start()
        for i in range(half):
            gown[i] = gram_of(side * half + i)
        for i in range(half):
            swap(i).wait_recv()
        for i in range(half):
            g = gown[i] + grecv[i]
            turned = g.T
            odd = g - turned
            pair = (sh[i], sl[i])
            once = dot_split(split(odd), pair)
            twice = dot_split(split(2.0 * (g + turned) - once - 0.5 * once.T), pair)
            x = odd - twice
            upper = x[:LANES, :LANES]
            lower = x[LANES:, LANES:]
            corner = jnp.where(row < column, upper - upper.T, lower - lower.T)
            packed = jnp.concatenate([corner, x[:LANES, LANES:] - x[LANES:, :LANES].T], axis=1)
            for h in range(2):
                for q in range(n_line):
                    at = (h * n_line + q) * piece
                    pk[i, h, q] = packed[at:at + piece]
        for i in range(half):
            cross(i).start()
    else:
        for b in range(blocks):
            grad_ref[b] = gram_of(b)

    if last:
        rotate(last)
        start_first(last)
    start_second(last)

    if own_gram:
        for i in range(half):
            cross(i).wait_recv()
            hsum[i] = pk[i, mine] + arecv[i]
            for o in range(1, n_line):
                along(i, o).start()

        places = []
        for b in range(blocks):
            place = owner_ref[b] * SLOTS
            for e in range(b):
                place = place + jnp.where(owner_ref[e] == owner_ref[b], 1, 0)
            places.append(place)

        def locate(q, _):
            found = jnp.int32(0)
            count = jnp.float32(0.0)
            for b in range(blocks):
                found = jnp.where(places[b] == q, b, found)
                count = jnp.where(places[b] == q, 1.0, count)
            idx_ref[q] = found
            valid_ref[q] = count
            return 0

        lax.fori_loop(0, n_dp * SLOTS, locate, 0)

        for i in range(half):
            total = hsum[i, line]
            for o in range(1, n_line):
                along(i, o).wait_recv()
                total = total + zrecv[i, o - 1]
            for h in range(2):
                gp[h, i] = total[:, h * LANES:(h + 1) * LANES]
        for k in range(3):
            trade(k).start()
        for k in range(3):
            trade(k).wait_recv()
        for i in range(half):
            gfull[side * half + i] = gp[side, i] + ax[1, i]
            gfull[(1 - side) * half + i] = ax[0, i] + ax[2, i]
        for d in range(n_dp):
            for s in range(SLOTS):
                slot_out[d, s] = gfull[idx_ref[d * SLOTS + s]] * valid_ref[d * SLOTS + s]
        for o in range(1, n_dp):
            deliver(o).start()
        slot_in[side, dp] = slot_out[dp]
        for j in range(last):
            finish(j)
        for o in range(1, n_dp):
            deliver(o).wait_recv()
        share.start()
        share.wait_recv()
        scale = 1.0 / math.sqrt(tokens * n_dp)
        for s in range(SLOTS):
            whole = []
            for h in range(2):
                rows = []
                for p in range(n_dp):
                    source = 2 * (p % n_line) + lax.rem(p // n_line + group, 2)
                    rows.append(slot_in[h, source, s])
                whole.append(jnp.concatenate(rows, axis=0) * scale)
            corner, beside = whole
            upper = jnp.where(row < column, corner, 0.0)
            lower = jnp.where(row > column, corner, 0.0)
            grad_ref[s, :LANES, :LANES] = upper - upper.T
            grad_ref[s, LANES:, LANES:] = lower - lower.T
            grad_ref[s, :LANES, LANES:] = beside
            grad_ref[s, LANES:, :LANES] = -beside.T
        finish(last)
        for i in range(half):
            swap(i).wait_send()
            cross(i).wait_send()
            for o in range(1, n_line):
                along(i, o).wait_send()
        for k in range(3):
            trade(k).wait_send()
        for o in range(1, n_dp):
            deliver(o).wait_send()
        share.wait_send()
    else:
        for j in range(last + 1):
            finish(j)
    for i in range(half):
        tell(i).wait_send()
    for j in range(last + 1):
        for i in range(per):
            for o in range(half_mp):
                first(j, o, i).wait_send()
            for o in range(1, half_mp):
                second(j, o, i).wait_send()


def publish(first, second):
    def body(a_ref, b_ref, oa_ref, ob_ref, sems):
        one = pltpu.make_async_copy(a_ref, oa_ref, sems.at[0])
        two = pltpu.make_async_copy(b_ref, ob_ref, sems.at[1])
        one.start()
        two.start()
        one.wait()
        two.wait()

    vmem = pl.BlockSpec(memory_space=pltpu.VMEM)
    hbm = pl.BlockSpec(memory_space=pl.ANY)
    return pl.pallas_call(
        body,
        out_shape=(jax.ShapeDtypeStruct(first.shape, first.dtype), jax.ShapeDtypeStruct(second.shape, second.dtype)),
        in_specs=[vmem, vmem],
        out_specs=(hbm, hbm),
        scratch_shapes=[pltpu.SemaphoreType.DMA((2,))],
        compiler_params=pltpu.CompilerParams(vmem_limit_bytes=2 * 1024 * 1024),
    )(first, second)


def local(n_dp, n_mp, activations, cotangent, frozen_weight, skew_params, tile_order, block_owner):
    tokens, dim = activations.shape
    hidden = cotangent.shape[1]
    blocks, block, _ = skew_params.shape
    tiles = tile_order.shape[0]
    piece = block // 2 // n_dp
    own_gram = piece * n_dp * 2 == block and piece % 8 == 0 and n_dp % 2 == 0 and n_mp == 4 and block == 2 * LANES
    keep = piece if own_gram else 8
    ring = n_dp if own_gram else 2
    half = blocks // 2
    some = half if own_gram else 1
    n_line = ring // 2
    half_mp = n_mp // 2
    per = tiles // n_mp
    span = max(half_mp - 1, 1)
    sizes = [z - a for a, z in cuts(tokens)]
    count = len(sizes)

    cfg = (tokens, dim, block, blocks, tiles, n_dp, n_mp, own_gram)
    smem = pl.BlockSpec(memory_space=pltpu.SMEM)
    vmem = pl.BlockSpec(memory_space=pltpu.VMEM)
    dma = pltpu.SemaphoreType.DMA
    grad_shape = (SLOTS if own_gram else blocks, block, block)
    squares = pltpu.VMEM((half, block, block), F32)
    gram = pltpu.VMEM((some, block, block), F32)

    def by_chunk(*lead):
        return tuple(pltpu.VMEM((*lead, rows, LANES), F32) for rows in sizes)

    input_grad, grads = pl.pallas_call(
        functools.partial(kernel, cfg),
        out_shape=(jax.ShapeDtypeStruct((tokens, dim // n_mp), BF16), jax.ShapeDtypeStruct(grad_shape, F32)),
        in_specs=[smem] * 2 + [pl.BlockSpec(memory_space=pl.ANY)] * 4,
        out_specs=(vmem, vmem),
        scratch_shapes=[
            pltpu.SMEM((tiles,), jnp.int32),
            pltpu.SMEM((n_dp * SLOTS,), jnp.int32),
            pltpu.SMEM((n_dp * SLOTS,), F32),
            pltpu.VMEM((hidden, tokens), BF16),
            pltpu.VMEM((tokens, hidden), BF16),
            pltpu.VMEM((hidden, dim), BF16),
            pltpu.VMEM((blocks, block, block), BF16),
            pltpu.VMEM((tiles, tokens, LANES), BF16),
            pltpu.VMEM((tiles, tokens, LANES), F32),
            by_chunk(tiles),
            by_chunk(half_mp, per),
            by_chunk(half_mp, per),
            by_chunk(span, per),
            by_chunk(span, per),
            pltpu.VMEM((half, block, block), BF16),
            pltpu.VMEM((half, block, block), BF16),
            pltpu.VMEM((blocks, block, block), BF16),
            pltpu.VMEM((blocks, block, block), BF16),
            squares, squares,
            gram, gram, gram,
            pltpu.VMEM((some, 2, n_line, keep, block), F32),
            pltpu.VMEM((some, n_line, keep, block), F32),
            pltpu.VMEM((some, n_line, keep, block), F32),
            pltpu.VMEM((some, max(n_line - 1, 1), keep, block), F32),
            pltpu.VMEM((2, some, keep, LANES), F32),
            pltpu.VMEM((3, some, keep, LANES), F32),
            pltpu.VMEM((2 * some, keep, LANES), F32),
            pltpu.VMEM((ring, SLOTS, keep, LANES), F32),
            pltpu.VMEM((2, ring, SLOTS, keep, LANES), F32),
            dma((blocks,)), dma((tiles,)), dma((2,)),
            dma((half,)), dma((half,)),
            dma((count, half_mp, per)), dma((count, half_mp, per)),
            dma((count, span, per)), dma((count, span, per)),
            dma((half,)), dma((half,)),
            dma((half,)), dma((half,)),
            dma((half, max(n_line - 1, 1))), dma((half, max(n_line - 1, 1))),
            dma((3,)), dma((3,)),
            dma((ring,)), dma((ring,)),
            dma((1,)), dma((1,)),
        ],
        compiler_params=pltpu.CompilerParams(
            collective_id=0, has_side_effects=True, vmem_limit_bytes=54 * 1024 * 1024),
    )(tile_order, block_owner, activations, cotangent.T, frozen_weight.T, skew_params)
    if own_gram:
        return publish(input_grad, grads)
    numbers = jnp.arange(blocks, dtype=jnp.int32)
    same = block_owner[:, None] == block_owner[None, :]
    rank = jnp.sum((same & (numbers[:, None] > numbers[None, :])).astype(jnp.int32), axis=1)
    place = block_owner * SLOTS + rank
    chosen = place[None, :] == jnp.arange(n_dp * SLOTS, dtype=jnp.int32)[:, None]
    index = jnp.sum(jnp.where(chosen, numbers[None, :], 0), axis=1)
    valid = jnp.sum(chosen.astype(F32), axis=1)
    gram = lax.psum(grads, ("dp", "mp"))
    at = lax.axis_index("dp") * SLOTS
    mine = lax.dynamic_slice(index, (at,), (SLOTS,))
    used = lax.dynamic_slice(valid, (at,), (SLOTS,))
    g = jnp.take(gram, mine, axis=0) * used[:, None, None]
    plain = jnp.take(skew_params, mine, axis=0).astype(F32)
    qt = jnp.swapaxes(plain, 1, 2) - plain
    mul = functools.partial(jnp.einsum, "bij,bjk->bik", precision=lax.Precision.HIGHEST)
    left = mul(g, qt)
    both = left + mul(qt, g)
    total = 2.0 * g + 2.0 * both + mul(left, qt) + mul(qt, both)
    return input_grad, (total - jnp.swapaxes(total, 1, 2)) * (1.0 / math.sqrt(tokens * n_dp))


def solution(mesh):
    placed = (P("dp", None), P("dp", "mp"), P(None, "mp"), P(), P(), P())
    return jax.shard_map(
        functools.partial(local, mesh.shape["dp"], mesh.shape["mp"]),
        mesh=mesh,
        in_specs=placed,
        out_specs=(P("dp", "mp"), P("dp", None, None)),
        check_vma=False,
    )
```

```python
import functools
import math

import jax
import jax.numpy as jnp
from jax import lax
from jax.experimental import pallas as pl
from jax.experimental.pallas import tpu as pltpu
from jax.sharding import PartitionSpec as P

SLOTS = 3
AHEAD = 4
LANES = 128
MESH = pl.DeviceIdType.MESH
F32 = jnp.float32
BF16 = jnp.bfloat16

NN = (((1,), (0,)), ((), ()))
TN = (((0,), (0,)), ((), ()))


def dot(a, b, dims=NN):
    return lax.dot_general(a, b, dims, preferred_element_type=F32)


def split(x):
    high = x.astype(BF16)
    return high, (x - high.astype(F32)).astype(BF16)


def dot_split(a, b):
    return dot(a[0], b[0]) + (dot(a[0], b[1]) + dot(a[1], b[0]))


def skew_of(params):
    plain = params.astype(F32)
    return plain - plain.T


def cuts(tokens):
    first = tokens * 3 // 8 // 16 * 16
    return ((0, first), (first, tokens)) if first else ((0, tokens),)


def kernel(cfg, order_hbm, owner_hbm, act_hbm, cot_hbm, w_hbm, s_hbm, out_ref, grad_ref, *scratch):
    tokens, dim, block, blocks, tiles, n_dp, n_mp, own_gram = cfg
    (order_ref, owner_ref, inv_ref, idx_ref, valid_ref, cot_ref, cots, w_ref, s_ref, acts, feat, outblk, part, recv1, send2, recv2,
     sh, sl, eth, etl, esend, erecv, gsend, gown, grecv, pk, arecv, hsum, zrecv, gp, ax, gfull, slot_out, slot_in,
     lw, la, lo, es, er, s1, r1, s2, r2, gs, gr, xs, xr, ds, dr, ys, yr, ss, sr, ms, mr) = scratch
    half_mp = n_mp // 2
    half = blocks // 2
    per = tiles // n_mp
    chunks = cuts(tokens)
    last = len(chunks) - 1
    dp = lax.axis_index("dp")
    mp = lax.axis_index("mp")
    side = lax.rem(mp, 2)
    group = mp // 2
    mate = group * 2 + (1 - side)

    load_s = pltpu.make_async_copy(s_hbm, s_ref, lo.at[0])
    load_cot = pltpu.make_async_copy(cot_hbm, cot_ref, lo.at[1])

    def load_w(n):
        at = pl.ds(pl.multiple_of(n * block, block), block)
        return pltpu.make_async_copy(w_hbm.at[:, at], w_ref.at[:, at], lw.at[n])

    def load_act(k):
        return pltpu.make_async_copy(act_hbm.at[:, k * LANES:(k + 1) * LANES], acts.at[k], la.at[k])

    load_order = pltpu.make_async_copy(order_hbm, order_ref, lo.at[2])
    load_owner = pltpu.make_async_copy(owner_hbm, owner_ref, lo.at[3])
    load_s.start()
    load_order.start()
    load_owner.start()
    load_cot.start()
    for n in range(AHEAD):
        load_w(n).start()

    def same_side(offset):
        return lax.rem(group + offset, half_mp)

    barrier = pltpu.get_barrier_semaphore()
    peers = []
    for o in range(half_mp):
        for k in range(2):
            if o or k:
                peers.append((dp, same_side(o) * 2 + (side if k == 0 else 1 - side)))
    if own_gram:
        for o in range(1, n_dp):
            peers.append((lax.rem(dp + o, n_dp), mp))
        for k in range(2):
            peers.append((dp + 1 - 2 * lax.rem(dp, 2), (1 - group) * 2 + (side if k == 0 else 1 - side)))
    for peer in peers:
        pl.semaphore_signal(barrier, inc=1, device_id=peer, device_id_type=MESH)

    def invert(k, _):
        found = jnp.int32(0)
        for i in range(tiles):
            found = jnp.where(order_ref[i] == k, i, found)
        inv_ref[k] = found
        return 0

    load_order.wait()
    load_owner.wait()
    lax.fori_loop(0, tiles, invert, 0)

    def tell(i):
        return pltpu.make_async_remote_copy(
            src_ref=esend.at[i], dst_ref=erecv.at[i], send_sem=es.at[i], recv_sem=er.at[i],
            device_id=(dp, mate), device_id_type=MESH)

    load_s.wait()
    for i in range(half):
        b = side * half + i
        skew = skew_of(s_ref[b])
        pair = split(skew)
        sh[i], sl[i] = pair
        square = dot_split(pair, pair)
        cube = dot_split(split(square), pair)
        turned = 2.0 * square - 2.0 * skew - cube
        esend[i] = turned
        eth[b], etl[b] = split(turned)
    pl.semaphore_wait(barrier, len(peers))
    for i in range(half):
        tell(i).start()
    for n in range(AHEAD, blocks):
        load_w(n).start()
    for k in range(tiles):
        load_act(k).start()

    load_cot.wait()
    for i in range(tokens // LANES):
        cots[i * LANES:(i + 1) * LANES, :] = cot_ref[:, i * LANES:(i + 1) * LANES].T

    def feature(n, at):
        a, z = at
        f = dot(cots[a:z, :], w_ref[:, pl.ds(pl.multiple_of(n * block, block), block)])
        feat[2 * n, a:z] = f[:, :LANES]
        feat[2 * n + 1, a:z] = f[:, LANES:]

    def first_features(k, _):
        for u in range(2):
            load_w(2 * k + u).wait()
        for u in range(2):
            feature(2 * k + u, chunks[0])
        return 0

    def rotate(j):
        a, z = chunks[j]

        def body(k, _):
            for u in range(half):
                b = k * half + u
                f = jnp.concatenate([feat[order_ref[2 * b], a:z], feat[order_ref[2 * b + 1], a:z]], axis=1)
                high, low = split(f)
                out = f + (dot(high, eth[b]) + (dot(low, eth[b]) + dot(high, etl[b])))
                outblk[j][2 * b] = out[:, :LANES]
                outblk[j][2 * b + 1] = out[:, LANES:]
            return 0
        lax.fori_loop(0, 2, body, 0)

    def first(j, o, i):
        q = same_side(o)
        return pltpu.make_async_remote_copy(
            src_ref=part[j].at[q, i], dst_ref=recv1[j].at[q, i],
            send_sem=s1.at[j, o, i], recv_sem=r1.at[j, o, i],
            device_id=(dp, mate), device_id_type=MESH)

    def second(j, o, i):
        return pltpu.make_async_remote_copy(
            src_ref=send2[j].at[o - 1, i], dst_ref=recv2[j].at[o - 1, i],
            send_sem=s2.at[j, o - 1, i], recv_sem=r2.at[j, o - 1, i],
            device_id=(dp, same_side(o) * 2 + side), device_id_type=MESH)

    def start_first(j):
        for o in list(range(1, half_mp)) + [0]:
            q = same_side(o)
            for i in range(per):
                part[j][q, i] = outblk[j][inv_ref[(q * 2 + (1 - side)) * per + i]]
                first(j, o, i).start()

    def start_second(j):
        for o in range(1, half_mp):
            q = same_side(o)
            for i in range(per):
                first(j, o, i).wait_recv()
                send2[j][o - 1, i] = outblk[j][inv_ref[(q * 2 + side) * per + i]] + recv1[j][q, i]
                second(j, o, i).start()

    def finish(j):
        a, z = chunks[j]
        for i in range(per):
            first(j, 0, i).wait_recv()
            total = outblk[j][inv_ref[mp * per + i]] + recv1[j][group, i]
            for o in range(1, half_mp):
                second(j, o, i).wait_recv()
                total = total + recv2[j][o - 1, i]
            out_ref[a:z, i * LANES:(i + 1) * LANES] = total.astype(out_ref.dtype)

    def gram_of(b):
        t0 = order_ref[2 * b]
        t1 = order_ref[2 * b + 1]
        high, low = split(jnp.concatenate([feat[t0], feat[t1]], axis=1))
        x = jnp.concatenate([acts[t0], acts[t1]], axis=1)
        return dot(x, high, TN) + dot(x, low, TN)

    def swap(i):
        return pltpu.make_async_remote_copy(
            src_ref=gsend.at[i], dst_ref=grecv.at[i], send_sem=gs.at[i], recv_sem=gr.at[i],
            device_id=(dp, mate), device_id_type=MESH)

    lax.fori_loop(0, blocks // 2, first_features, 0)
    for i in range(half):
        tell(i).wait_recv()
        b = (1 - side) * half + i
        eth[b], etl[b] = split(erecv[i])
    rotate(0)
    start_first(0)
    for j in range(1, last + 1):
        for n in range(half):
            feature(n, chunks[j])
        start_second(j - 1)
        for n in range(half, blocks):
            feature(n, chunks[j])
    for k in range(tiles):
        load_act(k).wait()

    if own_gram:
        parity = lax.rem(dp, 2)
        line = dp // 2
        n_line = n_dp // 2
        piece = block // 2 // n_dp
        mine = lax.rem(parity + group, 2)
        across = dp + 1 - 2 * parity

        def cross(i):
            return pltpu.make_async_remote_copy(
                src_ref=pk.at[i, 1 - mine], dst_ref=arecv.at[i], send_sem=xs.at[i], recv_sem=xr.at[i],
                device_id=(across, mp), device_id_type=MESH)

        def along(i, o):
            to = lax.rem(line + o, n_line)
            return pltpu.make_async_remote_copy(
                src_ref=hsum.at[i, to], dst_ref=zrecv.at[i, o - 1],
                send_sem=ds.at[i, o - 1], recv_sem=dr.at[i, o - 1],
                device_id=(to * 2 + parity, mp), device_id_type=MESH)

        def trade(k):
            column = side if k == 1 else 1 - side
            to = (dp, mate) if k == 0 else (across, (1 - group) * 2 + column)
            return pltpu.make_async_remote_copy(
                src_ref=gp.at[column], dst_ref=ax.at[k], send_sem=ys.at[k], recv_sem=yr.at[k],
                device_id=to, device_id_type=MESH)

        def deliver(o):
            to = lax.rem(dp + o, n_dp)
            return pltpu.make_async_remote_copy(
                src_ref=slot_out.at[to], dst_ref=slot_in.at[side, dp],
                send_sem=ss.at[o], recv_sem=sr.at[o],
                device_id=(to, mp), device_id_type=MESH)

        share = pltpu.make_async_remote_copy(
            src_ref=slot_in.at[side], dst_ref=slot_in.at[side], send_sem=ms.at[0], recv_sem=mr.at[0],
            device_id=(dp, mate), device_id_type=MESH)

        row = lax.broadcasted_iota(jnp.int32, (LANES, LANES), 0)
        column = lax.broadcasted_iota(jnp.int32, (LANES, LANES), 1)

        for i in range(half):
            gsend[i] = gram_of((1 - side) * half + i)
            swap(i).start()
        for i in range(half):
            gown[i] = gram_of(side * half + i)
        for i in range(half):
            swap(i).wait_recv()
        for i in range(half):
            g = gown[i] + grecv[i]
            turned = g.T
            odd = g - turned
            pair = (sh[i], sl[i])
            once = dot_split(split(odd), pair)
            twice = dot_split(split(2.0 * (g + turned) - once - 0.5 * once.T), pair)
            x = odd - twice
            upper = x[:LANES, :LANES]
            lower = x[LANES:, LANES:]
            corner = jnp.where(row < column, upper - upper.T, lower - lower.T)
            packed = jnp.concatenate([corner, x[:LANES, LANES:] - x[LANES:, :LANES].T], axis=1)
            for h in range(2):
                for q in range(n_line):
                    at = (h * n_line + q) * piece
                    pk[i, h, q] = packed[at:at + piece]
        for i in range(half):
            cross(i).start()
    else:
        for b in range(blocks):
            grad_ref[b] = gram_of(b)

    if last:
        rotate(last)
        start_first(last)
    start_second(last)

    if own_gram:
        for i in range(half):
            cross(i).wait_recv()
            hsum[i] = pk[i, mine] + arecv[i]
            for o in range(1, n_line):
                along(i, o).start()

        places = []
        for b in range(blocks):
            place = owner_ref[b] * SLOTS
            for e in range(b):
                place = place + jnp.where(owner_ref[e] == owner_ref[b], 1, 0)
            places.append(place)

        def locate(q, _):
            found = jnp.int32(0)
            count = jnp.float32(0.0)
            for b in range(blocks):
                found = jnp.where(places[b] == q, b, found)
                count = jnp.where(places[b] == q, 1.0, count)
            idx_ref[q] = found
            valid_ref[q] = count
            return 0

        lax.fori_loop(0, n_dp * SLOTS, locate, 0)

        for i in range(half):
            total = hsum[i, line]
            for o in range(1, n_line):
                along(i, o).wait_recv()
                total = total + zrecv[i, o - 1]
            for h in range(2):
                gp[h, i] = total[:, h * LANES:(h + 1) * LANES]
        for k in range(3):
            trade(k).start()
        for k in range(3):
            trade(k).wait_recv()
        for i in range(half):
            gfull[side * half + i] = gp[side, i] + ax[1, i]
            gfull[(1 - side) * half + i] = ax[0, i] + ax[2, i]
        for d in range(n_dp):
            for s in range(SLOTS):
                slot_out[d, s] = gfull[idx_ref[d * SLOTS + s]] * valid_ref[d * SLOTS + s]
        for o in range(1, n_dp):
            deliver(o).start()
        slot_in[side, dp] = slot_out[dp]
        for j in range(last):
            finish(j)
        for o in range(1, n_dp):
            deliver(o).wait_recv()
        share.start()
        share.wait_recv()
        scale = 1.0 / math.sqrt(tokens * n_dp)
        for s in range(SLOTS):
            whole = []
            for h in range(2):
                rows = []
                for p in range(n_dp):
                    source = 2 * (p % n_line) + lax.rem(p // n_line + group, 2)
                    rows.append(slot_in[h, source, s])
                whole.append(jnp.concatenate(rows, axis=0) * scale)
            corner, beside = whole
            upper = jnp.where(row < column, corner, 0.0)
            lower = jnp.where(row > column, corner, 0.0)
            grad_ref[s, :LANES, :LANES] = upper - upper.T
            grad_ref[s, LANES:, LANES:] = lower - lower.T
            grad_ref[s, :LANES, LANES:] = beside
            grad_ref[s, LANES:, :LANES] = -beside.T
        finish(last)
        for i in range(half):
            swap(i).wait_send()
            cross(i).wait_send()
            for o in range(1, n_line):
                along(i, o).wait_send()
        for k in range(3):
            trade(k).wait_send()
        for o in range(1, n_dp):
            deliver(o).wait_send()
        share.wait_send()
    else:
        for j in range(last + 1):
            finish(j)
    for i in range(half):
        tell(i).wait_send()
    for j in range(last + 1):
        for i in range(per):
            for o in range(half_mp):
                first(j, o, i).wait_send()
            for o in range(1, half_mp):
                second(j, o, i).wait_send()


def publish(first, second):
    def body(a_ref, b_ref, oa_ref, ob_ref, sems):
        one = pltpu.make_async_copy(a_ref, oa_ref, sems.at[0])
        two = pltpu.make_async_copy(b_ref, ob_ref, sems.at[1])
        one.start()
        two.start()
        one.wait()
        two.wait()

    vmem = pl.BlockSpec(memory_space=pltpu.VMEM)
    hbm = pl.BlockSpec(memory_space=pl.ANY)
    return pl.pallas_call(
        body,
        out_shape=(jax.ShapeDtypeStruct(first.shape, first.dtype), jax.ShapeDtypeStruct(second.shape, second.dtype)),
        in_specs=[vmem, vmem],
        out_specs=(hbm, hbm),
        scratch_shapes=[pltpu.SemaphoreType.DMA((2,))],
        compiler_params=pltpu.CompilerParams(vmem_limit_bytes=2 * 1024 * 1024),
    )(first, second)


def local(n_dp, n_mp, activations, cotangent, frozen_weight, skew_params, tile_order, block_owner):
    tokens, dim = activations.shape
    hidden = cotangent.shape[1]
    blocks, block, _ = skew_params.shape
    tiles = tile_order.shape[0]
    piece = block // 2 // n_dp
    own_gram = piece * n_dp * 2 == block and piece % 8 == 0 and n_dp % 2 == 0 and n_mp == 4 and block == 2 * LANES
    keep = piece if own_gram else 8
    ring = n_dp if own_gram else 2
    half = blocks // 2
    some = half if own_gram else 1
    n_line = ring // 2
    half_mp = n_mp // 2
    per = tiles // n_mp
    span = max(half_mp - 1, 1)
    sizes = [z - a for a, z in cuts(tokens)]
    count = len(sizes)

    cfg = (tokens, dim, block, blocks, tiles, n_dp, n_mp, own_gram)
    vmem = pl.BlockSpec(memory_space=pltpu.VMEM)
    dma = pltpu.SemaphoreType.DMA
    grad_shape = (SLOTS if own_gram else blocks, block, block)
    squares = pltpu.VMEM((half, block, block), F32)
    gram = pltpu.VMEM((some, block, block), F32)

    def by_chunk(*lead):
        return tuple(pltpu.VMEM((*lead, rows, LANES), F32) for rows in sizes)

    input_grad, grads = pl.pallas_call(
        functools.partial(kernel, cfg),
        out_shape=(jax.ShapeDtypeStruct((tokens, dim // n_mp), BF16), jax.ShapeDtypeStruct(grad_shape, F32)),
        in_specs=[pl.BlockSpec(memory_space=pltpu.HBM)] * 2 + [pl.BlockSpec(memory_space=pl.ANY)] * 4,
        out_specs=(vmem, vmem),
        scratch_shapes=[
            pltpu.SMEM((tiles,), jnp.int32),
            pltpu.SMEM((blocks,), jnp.int32),
            pltpu.SMEM((tiles,), jnp.int32),
            pltpu.SMEM((n_dp * SLOTS,), jnp.int32),
            pltpu.SMEM((n_dp * SLOTS,), F32),
            pltpu.VMEM((hidden, tokens), BF16),
            pltpu.VMEM((tokens, hidden), BF16),
            pltpu.VMEM((hidden, dim), BF16),
            pltpu.VMEM((blocks, block, block), BF16),
            pltpu.VMEM((tiles, tokens, LANES), BF16),
            pltpu.VMEM((tiles, tokens, LANES), F32),
            by_chunk(tiles),
            by_chunk(half_mp, per),
            by_chunk(half_mp, per),
            by_chunk(span, per),
            by_chunk(span, per),
            pltpu.VMEM((half, block, block), BF16),
            pltpu.VMEM((half, block, block), BF16),
            pltpu.VMEM((blocks, block, block), BF16),
            pltpu.VMEM((blocks, block, block), BF16),
            squares, squares,
            gram, gram, gram,
            pltpu.VMEM((some, 2, n_line, keep, block), F32),
            pltpu.VMEM((some, n_line, keep, block), F32),
            pltpu.VMEM((some, n_line, keep, block), F32),
            pltpu.VMEM((some, max(n_line - 1, 1), keep, block), F32),
            pltpu.VMEM((2, some, keep, LANES), F32),
            pltpu.VMEM((3, some, keep, LANES), F32),
            pltpu.VMEM((2 * some, keep, LANES), F32),
            pltpu.VMEM((ring, SLOTS, keep, LANES), F32),
            pltpu.VMEM((2, ring, SLOTS, keep, LANES), F32),
            dma((blocks,)), dma((tiles,)), dma((4,)),
            dma((half,)), dma((half,)),
            dma((count, half_mp, per)), dma((count, half_mp, per)),
            dma((count, span, per)), dma((count, span, per)),
            dma((half,)), dma((half,)),
            dma((half,)), dma((half,)),
            dma((half, max(n_line - 1, 1))), dma((half, max(n_line - 1, 1))),
            dma((3,)), dma((3,)),
            dma((ring,)), dma((ring,)),
            dma((1,)), dma((1,)),
        ],
        compiler_params=pltpu.CompilerParams(
            collective_id=0, has_side_effects=True, vmem_limit_bytes=54 * 1024 * 1024),
    )(tile_order, block_owner, activations, cotangent.T, frozen_weight.T, skew_params)
    if own_gram:
        return publish(input_grad, grads)
    numbers = jnp.arange(blocks, dtype=jnp.int32)
    same = block_owner[:, None] == block_owner[None, :]
    rank = jnp.sum((same & (numbers[:, None] > numbers[None, :])).astype(jnp.int32), axis=1)
    place = block_owner * SLOTS + rank
    chosen = place[None, :] == jnp.arange(n_dp * SLOTS, dtype=jnp.int32)[:, None]
    index = jnp.sum(jnp.where(chosen, numbers[None, :], 0), axis=1)
    valid = jnp.sum(chosen.astype(F32), axis=1)
    gram = lax.psum(grads, ("dp", "mp"))
    at = lax.axis_index("dp") * SLOTS
    mine = lax.dynamic_slice(index, (at,), (SLOTS,))
    used = lax.dynamic_slice(valid, (at,), (SLOTS,))
    g = jnp.take(gram, mine, axis=0) * used[:, None, None]
    plain = jnp.take(skew_params, mine, axis=0).astype(F32)
    qt = jnp.swapaxes(plain, 1, 2) - plain
    mul = functools.partial(jnp.einsum, "bij,bjk->bik", precision=lax.Precision.HIGHEST)
    left = mul(g, qt)
    both = left + mul(qt, g)
    total = 2.0 * g + 2.0 * both + mul(left, qt) + mul(qt, both)
    return input_grad, (total - jnp.swapaxes(total, 1, 2)) * (1.0 / math.sqrt(tokens * n_dp))


def solution(mesh):
    placed = (P("dp", None), P("dp", "mp"), P(None, "mp"), P(), P(), P())
    return jax.shard_map(
        functools.partial(local, mesh.shape["dp"], mesh.shape["mp"]),
        mesh=mesh,
        in_specs=placed,
        out_specs=(P("dp", "mp"), P("dp", None, None)),
        check_vma=False,
    )
```

```python
import functools
import math

import jax
import jax.numpy as jnp
from jax import lax
from jax.experimental import pallas as pl
from jax.experimental.pallas import tpu as pltpu
from jax.sharding import PartitionSpec as P

SLOTS = 3
AHEAD = 4
LANES = 128
MESH = pl.DeviceIdType.MESH
F32 = jnp.float32
BF16 = jnp.bfloat16

NN = (((1,), (0,)), ((), ()))
TN = (((0,), (0,)), ((), ()))


def dot(a, b, dims=NN):
    return lax.dot_general(a, b, dims, preferred_element_type=F32)


def split(x):
    high = x.astype(BF16)
    return high, (x - high.astype(F32)).astype(BF16)


def dot_split(a, b):
    return dot(a[0], b[0]) + (dot(a[0], b[1]) + dot(a[1], b[0]))


def skew_of(params):
    plain = params.astype(F32)
    return plain - plain.T


def cuts(tokens):
    first = tokens * 3 // 8 // 16 * 16
    return ((0, first), (first, tokens)) if first else ((0, tokens),)


def kernel(cfg, index_ref, act_hbm, cot_hbm, w_hbm, s_hbm, out_ref, grad_ref, *scratch):
    tokens, dim, block, blocks, tiles, n_dp, n_mp, own_gram = cfg
    (inv_ref, idx_ref, valid_ref, cot_ref, cots, w_ref, s_ref, acts, feat, outblk, part, recv1, send2, recv2,
     sh, sl, eth, etl, esend, erecv, gsend, gown, grecv, pk, arecv, hsum, zrecv, gp, ax, gfull, slot_out, slot_in,
     lw, la, lo, es, er, s1, r1, s2, r2, gs, gr, xs, xr, ds, dr, ys, yr, ss, sr, ms, mr) = scratch
    half_mp = n_mp // 2
    half = blocks // 2
    per = tiles // n_mp
    chunks = cuts(tokens)
    last = len(chunks) - 1
    dp = lax.axis_index("dp")
    mp = lax.axis_index("mp")
    side = lax.rem(mp, 2)
    group = mp // 2
    mate = group * 2 + (1 - side)

    load_s = pltpu.make_async_copy(s_hbm, s_ref, lo.at[0])
    load_cot = pltpu.make_async_copy(cot_hbm, cot_ref, lo.at[1])

    def load_w(n):
        at = pl.ds(pl.multiple_of(n * block, block), block)
        return pltpu.make_async_copy(w_hbm.at[:, at], w_ref.at[:, at], lw.at[n])

    def load_act(k):
        return pltpu.make_async_copy(act_hbm.at[:, k * LANES:(k + 1) * LANES], acts.at[k], la.at[k])

    load_s.start()
    load_cot.start()
    for n in range(AHEAD):
        load_w(n).start()

    def same_side(offset):
        return lax.rem(group + offset, half_mp)

    barrier = pltpu.get_barrier_semaphore()
    peers = []
    for o in range(half_mp):
        for k in range(2):
            if o or k:
                peers.append((dp, same_side(o) * 2 + (side if k == 0 else 1 - side)))
    if own_gram:
        for o in range(1, n_dp):
            peers.append((lax.rem(dp + o, n_dp), mp))
        for k in range(2):
            peers.append((dp + 1 - 2 * lax.rem(dp, 2), (1 - group) * 2 + (side if k == 0 else 1 - side)))
    for peer in peers:
        pl.semaphore_signal(barrier, inc=1, device_id=peer, device_id_type=MESH)

    def invert(k, _):
        found = jnp.int32(0)
        for i in range(tiles):
            found = jnp.where(index_ref[i] == k, i, found)
        inv_ref[k] = found
        return 0


    lax.fori_loop(0, tiles, invert, 0)

    def tell(i):
        return pltpu.make_async_remote_copy(
            src_ref=esend.at[i], dst_ref=erecv.at[i], send_sem=es.at[i], recv_sem=er.at[i],
            device_id=(dp, mate), device_id_type=MESH)

    load_s.wait()
    for i in range(half):
        b = side * half + i
        skew = skew_of(s_ref[b])
        pair = split(skew)
        sh[i], sl[i] = pair
        square = dot_split(pair, pair)
        cube = dot_split(split(square), pair)
        turned = 2.0 * square - 2.0 * skew - cube
        esend[i] = turned
        eth[b], etl[b] = split(turned)
    pl.semaphore_wait(barrier, len(peers))
    for i in range(half):
        tell(i).start()
    for n in range(AHEAD, blocks):
        load_w(n).start()
    for k in range(tiles):
        load_act(k).start()

    load_cot.wait()
    for i in range(tokens // LANES):
        cots[i * LANES:(i + 1) * LANES, :] = cot_ref[:, i * LANES:(i + 1) * LANES].T

    def feature(n, at):
        a, z = at
        f = dot(cots[a:z, :], w_ref[:, pl.ds(pl.multiple_of(n * block, block), block)])
        feat[2 * n, a:z] = f[:, :LANES]
        feat[2 * n + 1, a:z] = f[:, LANES:]

    def first_features(k, _):
        for u in range(2):
            load_w(2 * k + u).wait()
        for u in range(2):
            feature(2 * k + u, chunks[0])
        return 0

    def rotate(j):
        a, z = chunks[j]

        def body(k, _):
            for u in range(half):
                b = k * half + u
                f = jnp.concatenate([feat[index_ref[2 * b], a:z], feat[index_ref[2 * b + 1], a:z]], axis=1)
                high, low = split(f)
                out = f + (dot(high, eth[b]) + (dot(low, eth[b]) + dot(high, etl[b])))
                outblk[j][2 * b] = out[:, :LANES]
                outblk[j][2 * b + 1] = out[:, LANES:]
            return 0
        lax.fori_loop(0, 2, body, 0)

    def first(j, o, i):
        q = same_side(o)
        return pltpu.make_async_remote_copy(
            src_ref=part[j].at[q, i], dst_ref=recv1[j].at[q, i],
            send_sem=s1.at[j, o, i], recv_sem=r1.at[j, o, i],
            device_id=(dp, mate), device_id_type=MESH)

    def second(j, o, i):
        return pltpu.make_async_remote_copy(
            src_ref=send2[j].at[o - 1, i], dst_ref=recv2[j].at[o - 1, i],
            send_sem=s2.at[j, o - 1, i], recv_sem=r2.at[j, o - 1, i],
            device_id=(dp, same_side(o) * 2 + side), device_id_type=MESH)

    def start_first(j):
        for o in list(range(1, half_mp)) + [0]:
            q = same_side(o)
            for i in range(per):
                part[j][q, i] = outblk[j][inv_ref[(q * 2 + (1 - side)) * per + i]]
                first(j, o, i).start()

    def start_second(j):
        for o in range(1, half_mp):
            q = same_side(o)
            for i in range(per):
                first(j, o, i).wait_recv()
                send2[j][o - 1, i] = outblk[j][inv_ref[(q * 2 + side) * per + i]] + recv1[j][q, i]
                second(j, o, i).start()

    def finish(j):
        a, z = chunks[j]
        for i in range(per):
            first(j, 0, i).wait_recv()
            total = outblk[j][inv_ref[mp * per + i]] + recv1[j][group, i]
            for o in range(1, half_mp):
                second(j, o, i).wait_recv()
                total = total + recv2[j][o - 1, i]
            out_ref[a:z, i * LANES:(i + 1) * LANES] = total.astype(out_ref.dtype)

    def gram_of(b):
        t0 = index_ref[2 * b]
        t1 = index_ref[2 * b + 1]
        high, low = split(jnp.concatenate([feat[t0], feat[t1]], axis=1))
        x = jnp.concatenate([acts[t0], acts[t1]], axis=1)
        return dot(x, high, TN) + dot(x, low, TN)

    def swap(i):
        return pltpu.make_async_remote_copy(
            src_ref=gsend.at[i], dst_ref=grecv.at[i], send_sem=gs.at[i], recv_sem=gr.at[i],
            device_id=(dp, mate), device_id_type=MESH)

    lax.fori_loop(0, blocks // 2, first_features, 0)
    for i in range(half):
        tell(i).wait_recv()
        b = (1 - side) * half + i
        eth[b], etl[b] = split(erecv[i])
    rotate(0)
    start_first(0)
    for j in range(1, last + 1):
        for n in range(half):
            feature(n, chunks[j])
        start_second(j - 1)
        for n in range(half, blocks):
            feature(n, chunks[j])
    for k in range(tiles):
        load_act(k).wait()

    if own_gram:
        parity = lax.rem(dp, 2)
        line = dp // 2
        n_line = n_dp // 2
        piece = block // 2 // n_dp
        mine = lax.rem(parity + group, 2)
        across = dp + 1 - 2 * parity

        def cross(i):
            return pltpu.make_async_remote_copy(
                src_ref=pk.at[i, 1 - mine], dst_ref=arecv.at[i], send_sem=xs.at[i], recv_sem=xr.at[i],
                device_id=(across, mp), device_id_type=MESH)

        def along(i, o):
            to = lax.rem(line + o, n_line)
            return pltpu.make_async_remote_copy(
                src_ref=hsum.at[i, to], dst_ref=zrecv.at[i, o - 1],
                send_sem=ds.at[i, o - 1], recv_sem=dr.at[i, o - 1],
                device_id=(to * 2 + parity, mp), device_id_type=MESH)

        def trade(k, i):
            column = side if k == 1 else 1 - side
            to = (dp, mate) if k == 0 else (across, (1 - group) * 2 + column)
            return pltpu.make_async_remote_copy(
                src_ref=gp.at[column, i], dst_ref=ax.at[k, i], send_sem=ys.at[k, i], recv_sem=yr.at[k, i],
                device_id=to, device_id_type=MESH)

        def deliver(o):
            to = lax.rem(dp + o, n_dp)
            return pltpu.make_async_remote_copy(
                src_ref=slot_out.at[to], dst_ref=slot_in.at[side, dp],
                send_sem=ss.at[o], recv_sem=sr.at[o],
                device_id=(to, mp), device_id_type=MESH)

        share = pltpu.make_async_remote_copy(
            src_ref=slot_in.at[side], dst_ref=slot_in.at[side], send_sem=ms.at[0], recv_sem=mr.at[0],
            device_id=(dp, mate), device_id_type=MESH)

        row = lax.broadcasted_iota(jnp.int32, (LANES, LANES), 0)
        column = lax.broadcasted_iota(jnp.int32, (LANES, LANES), 1)

        for i in range(half):
            gsend[i] = gram_of((1 - side) * half + i)
            swap(i).start()
        for i in range(half):
            gown[i] = gram_of(side * half + i)
        for i in range(half):
            swap(i).wait_recv()
        for i in range(half):
            g = gown[i] + grecv[i]
            turned = g.T
            odd = g - turned
            pair = (sh[i], sl[i])
            once = dot_split(split(odd), pair)
            twice = dot_split(split(2.0 * (g + turned) - once - 0.5 * once.T), pair)
            x = odd - twice
            upper = x[:LANES, :LANES]
            lower = x[LANES:, LANES:]
            corner = jnp.where(row < column, upper - upper.T, lower - lower.T)
            packed = jnp.concatenate([corner, x[:LANES, LANES:] - x[LANES:, :LANES].T], axis=1)
            for h in range(2):
                for q in range(n_line):
                    at = (h * n_line + q) * piece
                    pk[i, h, q] = packed[at:at + piece]
        for i in range(half):
            cross(i).start()
    else:
        for b in range(blocks):
            grad_ref[b] = gram_of(b)

    if last:
        rotate(last)
        start_first(last)
    start_second(last)

    if own_gram:
        for i in range(half):
            cross(i).wait_recv()
            hsum[i] = pk[i, mine] + arecv[i]
            for o in range(1, n_line):
                along(i, o).start()

        places = []
        for b in range(blocks):
            place = index_ref[tiles + b] * SLOTS
            for e in range(b):
                place = place + jnp.where(index_ref[tiles + e] == index_ref[tiles + b], 1, 0)
            places.append(place)

        def locate(q, _):
            found = jnp.int32(0)
            count = jnp.float32(0.0)
            for b in range(blocks):
                found = jnp.where(places[b] == q, b, found)
                count = jnp.where(places[b] == q, 1.0, count)
            idx_ref[q] = found
            valid_ref[q] = count
            return 0

        lax.fori_loop(0, n_dp * SLOTS, locate, 0)

        for i in range(half):
            total = hsum[i, line]
            for o in range(1, n_line):
                along(i, o).wait_recv()
                total = total + zrecv[i, o - 1]
            for h in range(2):
                gp[h, i] = total[:, h * LANES:(h + 1) * LANES]
            for k in range(3):
                trade(k, i).start()
        for i in range(half):
            for k in range(3):
                trade(k, i).wait_recv()
        for i in range(half):
            gfull[side * half + i] = gp[side, i] + ax[1, i]
            gfull[(1 - side) * half + i] = ax[0, i] + ax[2, i]
        for d in range(n_dp):
            for s in range(SLOTS):
                slot_out[d, s] = gfull[idx_ref[d * SLOTS + s]] * valid_ref[d * SLOTS + s]
        for o in range(1, n_dp):
            deliver(o).start()
        slot_in[side, dp] = slot_out[dp]
        for j in range(last):
            finish(j)
        for o in range(1, n_dp):
            deliver(o).wait_recv()
        share.start()
        share.wait_recv()
        scale = 1.0 / math.sqrt(tokens * n_dp)
        for s in range(SLOTS):
            whole = []
            for h in range(2):
                rows = []
                for p in range(n_dp):
                    source = 2 * (p % n_line) + lax.rem(p // n_line + group, 2)
                    rows.append(slot_in[h, source, s])
                whole.append(jnp.concatenate(rows, axis=0) * scale)
            corner, beside = whole
            upper = jnp.where(row < column, corner, 0.0)
            lower = jnp.where(row > column, corner, 0.0)
            grad_ref[s, :LANES, :LANES] = upper - upper.T
            grad_ref[s, LANES:, LANES:] = lower - lower.T
            grad_ref[s, :LANES, LANES:] = beside
            grad_ref[s, LANES:, :LANES] = -beside.T
        finish(last)
        for i in range(half):
            swap(i).wait_send()
            cross(i).wait_send()
            for o in range(1, n_line):
                along(i, o).wait_send()
            for k in range(3):
                trade(k, i).wait_send()
        for o in range(1, n_dp):
            deliver(o).wait_send()
        share.wait_send()
    else:
        for j in range(last + 1):
            finish(j)
    for i in range(half):
        tell(i).wait_send()
    for j in range(last + 1):
        for i in range(per):
            for o in range(half_mp):
                first(j, o, i).wait_send()
            for o in range(1, half_mp):
                second(j, o, i).wait_send()


def publish(first, second):
    def body(a_ref, b_ref, oa_ref, ob_ref, sems):
        one = pltpu.make_async_copy(a_ref, oa_ref, sems.at[0])
        two = pltpu.make_async_copy(b_ref, ob_ref, sems.at[1])
        one.start()
        two.start()
        one.wait()
        two.wait()

    vmem = pl.BlockSpec(memory_space=pltpu.VMEM)
    hbm = pl.BlockSpec(memory_space=pl.ANY)
    return pl.pallas_call(
        body,
        out_shape=(jax.ShapeDtypeStruct(first.shape, first.dtype), jax.ShapeDtypeStruct(second.shape, second.dtype)),
        in_specs=[vmem, vmem],
        out_specs=(hbm, hbm),
        scratch_shapes=[pltpu.SemaphoreType.DMA((2,))],
        compiler_params=pltpu.CompilerParams(vmem_limit_bytes=2 * 1024 * 1024),
    )(first, second)


def local(n_dp, n_mp, activations, cotangent, frozen_weight, skew_params, tile_order, block_owner):
    tokens, dim = activations.shape
    hidden = cotangent.shape[1]
    blocks, block, _ = skew_params.shape
    tiles = tile_order.shape[0]
    piece = block // 2 // n_dp
    own_gram = piece * n_dp * 2 == block and piece % 8 == 0 and n_dp % 2 == 0 and n_mp == 4 and block == 2 * LANES
    keep = piece if own_gram else 8
    ring = n_dp if own_gram else 2
    half = blocks // 2
    some = half if own_gram else 1
    n_line = ring // 2
    half_mp = n_mp // 2
    per = tiles // n_mp
    span = max(half_mp - 1, 1)
    sizes = [z - a for a, z in cuts(tokens)]
    count = len(sizes)

    cfg = (tokens, dim, block, blocks, tiles, n_dp, n_mp, own_gram)
    vmem = pl.BlockSpec(memory_space=pltpu.VMEM)
    dma = pltpu.SemaphoreType.DMA
    grad_shape = (SLOTS if own_gram else blocks, block, block)
    squares = pltpu.VMEM((half, block, block), F32)
    gram = pltpu.VMEM((some, block, block), F32)

    def by_chunk(*lead):
        return tuple(pltpu.VMEM((*lead, rows, LANES), F32) for rows in sizes)

    input_grad, grads = pl.pallas_call(
        functools.partial(kernel, cfg),
        out_shape=(jax.ShapeDtypeStruct((tokens, dim // n_mp), BF16), jax.ShapeDtypeStruct(grad_shape, F32)),
        in_specs=[pl.BlockSpec(memory_space=pltpu.SMEM)] + [pl.BlockSpec(memory_space=pl.ANY)] * 4,
        out_specs=(vmem, vmem),
        scratch_shapes=[
            pltpu.SMEM((tiles,), jnp.int32),
            pltpu.SMEM((n_dp * SLOTS,), jnp.int32),
            pltpu.SMEM((n_dp * SLOTS,), F32),
            pltpu.VMEM((hidden, tokens), BF16),
            pltpu.VMEM((tokens, hidden), BF16),
            pltpu.VMEM((hidden, dim), BF16),
            pltpu.VMEM((blocks, block, block), BF16),
            pltpu.VMEM((tiles, tokens, LANES), BF16),
            pltpu.VMEM((tiles, tokens, LANES), F32),
            by_chunk(tiles),
            by_chunk(half_mp, per),
            by_chunk(half_mp, per),
            by_chunk(span, per),
            by_chunk(span, per),
            pltpu.VMEM((half, block, block), BF16),
            pltpu.VMEM((half, block, block), BF16),
            pltpu.VMEM((blocks, block, block), BF16),
            pltpu.VMEM((blocks, block, block), BF16),
            squares, squares,
            gram, gram, gram,
            pltpu.VMEM((some, 2, n_line, keep, block), F32),
            pltpu.VMEM((some, n_line, keep, block), F32),
            pltpu.VMEM((some, n_line, keep, block), F32),
            pltpu.VMEM((some, max(n_line - 1, 1), keep, block), F32),
            pltpu.VMEM((2, some, keep, LANES), F32),
            pltpu.VMEM((3, some, keep, LANES), F32),
            pltpu.VMEM((2 * some, keep, LANES), F32),
            pltpu.VMEM((ring, SLOTS, keep, LANES), F32),
            pltpu.VMEM((2, ring, SLOTS, keep, LANES), F32),
            dma((blocks,)), dma((tiles,)), dma((2,)),
            dma((half,)), dma((half,)),
            dma((count, half_mp, per)), dma((count, half_mp, per)),
            dma((count, span, per)), dma((count, span, per)),
            dma((half,)), dma((half,)),
            dma((half,)), dma((half,)),
            dma((half, max(n_line - 1, 1))), dma((half, max(n_line - 1, 1))),
            dma((3, half)), dma((3, half)),
            dma((ring,)), dma((ring,)),
            dma((1,)), dma((1,)),
        ],
        compiler_params=pltpu.CompilerParams(
            collective_id=0, has_side_effects=True, vmem_limit_bytes=52 * 1024 * 1024),
    )(jnp.concatenate([tile_order, block_owner]), activations, cotangent.T, frozen_weight.T, skew_params)
    if own_gram:
        return publish(input_grad, grads)
    numbers = jnp.arange(blocks, dtype=jnp.int32)
    same = block_owner[:, None] == block_owner[None, :]
    rank = jnp.sum((same & (numbers[:, None] > numbers[None, :])).astype(jnp.int32), axis=1)
    place = block_owner * SLOTS + rank
    chosen = place[None, :] == jnp.arange(n_dp * SLOTS, dtype=jnp.int32)[:, None]
    index = jnp.sum(jnp.where(chosen, numbers[None, :], 0), axis=1)
    valid = jnp.sum(chosen.astype(F32), axis=1)
    gram = lax.psum(grads, ("dp", "mp"))
    at = lax.axis_index("dp") * SLOTS
    mine = lax.dynamic_slice(index, (at,), (SLOTS,))
    used = lax.dynamic_slice(valid, (at,), (SLOTS,))
    g = jnp.take(gram, mine, axis=0) * used[:, None, None]
    plain = jnp.take(skew_params, mine, axis=0).astype(F32)
    qt = jnp.swapaxes(plain, 1, 2) - plain
    mul = functools.partial(jnp.einsum, "bij,bjk->bik", precision=lax.Precision.HIGHEST)
    left = mul(g, qt)
    both = left + mul(qt, g)
    total = 2.0 * g + 2.0 * both + mul(left, qt) + mul(qt, both)
    return input_grad, (total - jnp.swapaxes(total, 1, 2)) * (1.0 / math.sqrt(tokens * n_dp))


def solution(mesh):
    placed = (P("dp", None), P("dp", "mp"), P(None, "mp"), P(), P(), P())
    return jax.shard_map(
        functools.partial(local, mesh.shape["dp"], mesh.shape["mp"]),
        mesh=mesh,
        in_specs=placed,
        out_specs=(P("dp", "mp"), P("dp", None, None)),
        check_vma=False,
    )
```

```python
import functools
import math

import jax
import jax.numpy as jnp
from jax import lax
from jax.experimental import pallas as pl
from jax.experimental.pallas import tpu as pltpu
from jax.sharding import PartitionSpec as P

SLOTS = 3
AHEAD = 4
LANES = 128
MESH = pl.DeviceIdType.MESH
F32 = jnp.float32
BF16 = jnp.bfloat16

NN = (((1,), (0,)), ((), ()))
TN = (((0,), (0,)), ((), ()))


def dot(a, b, dims=NN):
    return lax.dot_general(a, b, dims, preferred_element_type=F32)


def split(x):
    high = x.astype(BF16)
    return high, (x - high.astype(F32)).astype(BF16)


def dot_split(a, b):
    return dot(a[0], b[0]) + (dot(a[0], b[1]) + dot(a[1], b[0]))


def skew_of(params):
    plain = params.astype(F32)
    return plain - plain.T


def cuts(tokens):
    first = tokens * 3 // 8 // 16 * 16
    return ((0, first), (first, tokens)) if first else ((0, tokens),)


def kernel(cfg, index_ref, act_hbm, cot_hbm, w_hbm, s_hbm, out_ref, grad_ref, *scratch):
    tokens, dim, block, blocks, tiles, n_dp, n_mp, own_gram = cfg
    (inv_ref, idx_ref, valid_ref, cot_ref, cots, w_ref, s_ref, acts, feat, outblk, part, recv1, send2, recv2,
     sh, sl, eth, etl, esend, erecv, gsend, gown, grecv, pk, arecv, hsum, zrecv, gp, ax, gfull, slot_out, slot_in,
     lw, la, lo, es, er, s1, r1, s2, r2, gs, gr, xs, xr, ds, dr, ys, yr, ss, sr, ms, mr) = scratch
    half_mp = n_mp // 2
    half = blocks // 2
    per = tiles // n_mp
    chunks = cuts(tokens)
    last = len(chunks) - 1
    dp = lax.axis_index("dp")
    mp = lax.axis_index("mp")
    side = lax.rem(mp, 2)
    group = mp // 2
    mate = group * 2 + (1 - side)

    load_s = pltpu.make_async_copy(s_hbm, s_ref, lo.at[0])
    load_cot = pltpu.make_async_copy(cot_hbm, cot_ref, lo.at[1])

    def load_w(n):
        at = pl.ds(pl.multiple_of(n * block, block), block)
        return pltpu.make_async_copy(w_hbm.at[:, at], w_ref.at[:, at], lw.at[n])

    def load_act(k):
        return pltpu.make_async_copy(act_hbm.at[:, k * LANES:(k + 1) * LANES], acts.at[k], la.at[k])

    load_s.start()
    load_cot.start()
    for n in range(AHEAD):
        load_w(n).start()

    def same_side(offset):
        return lax.rem(group + offset, half_mp)

    barrier = pltpu.get_barrier_semaphore()
    peers = []
    for o in range(half_mp):
        for k in range(2):
            if o or k:
                peers.append((dp, same_side(o) * 2 + (side if k == 0 else 1 - side)))
    if own_gram:
        for o in range(1, n_dp):
            peers.append((lax.rem(dp + o, n_dp), mp))
        for k in range(2):
            peers.append((dp + 1 - 2 * lax.rem(dp, 2), (1 - group) * 2 + (side if k == 0 else 1 - side)))
    for peer in peers:
        pl.semaphore_signal(barrier, inc=1, device_id=peer, device_id_type=MESH)

    def invert(k, _):
        found = jnp.int32(0)
        for i in range(tiles):
            found = jnp.where(index_ref[i] == k, i, found)
        inv_ref[k] = found
        return 0


    lax.fori_loop(0, tiles, invert, 0)

    def tell(i):
        return pltpu.make_async_remote_copy(
            src_ref=esend.at[i], dst_ref=erecv.at[i], send_sem=es.at[i], recv_sem=er.at[i],
            device_id=(dp, mate), device_id_type=MESH)

    load_s.wait()
    for i in range(half):
        b = side * half + i
        skew = skew_of(s_ref[b])
        pair = split(skew)
        sh[i], sl[i] = pair
        square = dot_split(pair, pair)
        cube = dot_split(split(square), pair)
        turned = 2.0 * square - 2.0 * skew - cube
        esend[i] = turned
        eth[b], etl[b] = split(turned)
    pl.semaphore_wait(barrier, len(peers))
    for i in range(half):
        tell(i).start()
    for n in range(AHEAD, blocks):
        load_w(n).start()

    load_cot.wait()
    for i in range(tokens // LANES):
        cots[i * LANES:(i + 1) * LANES, :] = cot_ref[:, i * LANES:(i + 1) * LANES].T

    def feature(n, at):
        a, z = at
        f = dot(cots[a:z, :], w_ref[:, pl.ds(pl.multiple_of(n * block, block), block)])
        feat[2 * n, a:z] = f[:, :LANES]
        feat[2 * n + 1, a:z] = f[:, LANES:]

    def first_features(k, _):
        for u in range(2):
            load_w(2 * k + u).wait()
        for u in range(2):
            feature(2 * k + u, chunks[0])
        return 0

    def rotate(j):
        a, z = chunks[j]

        def body(k, _):
            for u in range(half):
                b = k * half + u
                f = jnp.concatenate([feat[index_ref[2 * b], a:z], feat[index_ref[2 * b + 1], a:z]], axis=1)
                high, low = split(f)
                out = f + (dot(high, eth[b]) + (dot(low, eth[b]) + dot(high, etl[b])))
                outblk[j][2 * b] = out[:, :LANES]
                outblk[j][2 * b + 1] = out[:, LANES:]
            return 0
        lax.fori_loop(0, 2, body, 0)

    def first(j, o, i):
        q = same_side(o)
        return pltpu.make_async_remote_copy(
            src_ref=part[j].at[q, i], dst_ref=recv1[j].at[q, i],
            send_sem=s1.at[j, o, i], recv_sem=r1.at[j, o, i],
            device_id=(dp, mate), device_id_type=MESH)

    def second(j, o, i):
        return pltpu.make_async_remote_copy(
            src_ref=send2[j].at[o - 1, i], dst_ref=recv2[j].at[o - 1, i],
            send_sem=s2.at[j, o - 1, i], recv_sem=r2.at[j, o - 1, i],
            device_id=(dp, same_side(o) * 2 + side), device_id_type=MESH)

    def start_first(j):
        for o in list(range(1, half_mp)) + [0]:
            q = same_side(o)
            for i in range(per):
                part[j][q, i] = outblk[j][inv_ref[(q * 2 + (1 - side)) * per + i]]
                first(j, o, i).start()

    def start_second(j):
        for o in range(1, half_mp):
            q = same_side(o)
            for i in range(per):
                first(j, o, i).wait_recv()
                send2[j][o - 1, i] = outblk[j][inv_ref[(q * 2 + side) * per + i]] + recv1[j][q, i]
                second(j, o, i).start()

    def finish(j):
        a, z = chunks[j]
        for i in range(per):
            first(j, 0, i).wait_recv()
            total = outblk[j][inv_ref[mp * per + i]] + recv1[j][group, i]
            for o in range(1, half_mp):
                second(j, o, i).wait_recv()
                total = total + recv2[j][o - 1, i]
            out_ref[a:z, i * LANES:(i + 1) * LANES] = total.astype(out_ref.dtype)

    def gram_of(b):
        t0 = index_ref[2 * b]
        t1 = index_ref[2 * b + 1]
        high, low = split(jnp.concatenate([feat[t0], feat[t1]], axis=1))
        x = jnp.concatenate([acts[t0], acts[t1]], axis=1)
        return dot(x, high, TN) + dot(x, low, TN)

    def swap(i):
        return pltpu.make_async_remote_copy(
            src_ref=gsend.at[i], dst_ref=grecv.at[i], send_sem=gs.at[i], recv_sem=gr.at[i],
            device_id=(dp, mate), device_id_type=MESH)

    lax.fori_loop(0, blocks // 2, first_features, 0)
    for i in range(half):
        tell(i).wait_recv()
        b = (1 - side) * half + i
        eth[b], etl[b] = split(erecv[i])
    rotate(0)
    start_first(0)
    for k in range(tiles):
        load_act(k).start()
    for j in range(1, last + 1):
        for n in range(half):
            feature(n, chunks[j])
        start_second(j - 1)
        for n in range(half, blocks):
            feature(n, chunks[j])
    for k in range(tiles):
        load_act(k).wait()

    if own_gram:
        parity = lax.rem(dp, 2)
        line = dp // 2
        n_line = n_dp // 2
        piece = block // 2 // n_dp
        mine = lax.rem(parity + group, 2)
        across = dp + 1 - 2 * parity

        def cross(i):
            return pltpu.make_async_remote_copy(
                src_ref=pk.at[i, 1 - mine], dst_ref=arecv.at[i], send_sem=xs.at[i], recv_sem=xr.at[i],
                device_id=(across, mp), device_id_type=MESH)

        def along(i, o):
            to = lax.rem(line + o, n_line)
            return pltpu.make_async_remote_copy(
                src_ref=hsum.at[i, to], dst_ref=zrecv.at[i, o - 1],
                send_sem=ds.at[i, o - 1], recv_sem=dr.at[i, o - 1],
                device_id=(to * 2 + parity, mp), device_id_type=MESH)

        def trade(k, i):
            column = side if k == 1 else 1 - side
            to = (dp, mate) if k == 0 else (across, (1 - group) * 2 + column)
            return pltpu.make_async_remote_copy(
                src_ref=gp.at[column, i], dst_ref=ax.at[k, i], send_sem=ys.at[k, i], recv_sem=yr.at[k, i],
                device_id=to, device_id_type=MESH)

        def deliver(o):
            to = lax.rem(dp + o, n_dp)
            return pltpu.make_async_remote_copy(
                src_ref=slot_out.at[to], dst_ref=slot_in.at[side, dp],
                send_sem=ss.at[o], recv_sem=sr.at[o],
                device_id=(to, mp), device_id_type=MESH)

        share = pltpu.make_async_remote_copy(
            src_ref=slot_in.at[side], dst_ref=slot_in.at[side], send_sem=ms.at[0], recv_sem=mr.at[0],
            device_id=(dp, mate), device_id_type=MESH)

        row = lax.broadcasted_iota(jnp.int32, (LANES, LANES), 0)
        column = lax.broadcasted_iota(jnp.int32, (LANES, LANES), 1)

        for i in range(half):
            gsend[i] = gram_of((1 - side) * half + i)
            swap(i).start()
        for i in range(half):
            gown[i] = gram_of(side * half + i)
        for i in range(half):
            swap(i).wait_recv()
        for i in range(half):
            g = gown[i] + grecv[i]
            turned = g.T
            odd = g - turned
            pair = (sh[i], sl[i])
            once = dot_split(split(odd), pair)
            twice = dot_split(split(2.0 * (g + turned) - once - 0.5 * once.T), pair)
            x = odd - twice
            upper = x[:LANES, :LANES]
            lower = x[LANES:, LANES:]
            corner = jnp.where(row < column, upper - upper.T, lower - lower.T)
            packed = jnp.concatenate([corner, x[:LANES, LANES:] - x[LANES:, :LANES].T], axis=1)
            for h in range(2):
                for q in range(n_line):
                    at = (h * n_line + q) * piece
                    pk[i, h, q] = packed[at:at + piece]
        for i in range(half):
            cross(i).start()
    else:
        for b in range(blocks):
            grad_ref[b] = gram_of(b)

    if last:
        rotate(last)
        start_first(last)
    start_second(last)

    if own_gram:
        for i in range(half):
            cross(i).wait_recv()
            hsum[i] = pk[i, mine] + arecv[i]
            for o in range(1, n_line):
                along(i, o).start()

        places = []
        for b in range(blocks):
            place = index_ref[tiles + b] * SLOTS
            for e in range(b):
                place = place + jnp.where(index_ref[tiles + e] == index_ref[tiles + b], 1, 0)
            places.append(place)

        def locate(q, _):
            found = jnp.int32(0)
            count = jnp.float32(0.0)
            for b in range(blocks):
                found = jnp.where(places[b] == q, b, found)
                count = jnp.where(places[b] == q, 1.0, count)
            idx_ref[q] = found
            valid_ref[q] = count
            return 0

        lax.fori_loop(0, n_dp * SLOTS, locate, 0)

        for i in range(half):
            total = hsum[i, line]
            for o in range(1, n_line):
                along(i, o).wait_recv()
                total = total + zrecv[i, o - 1]
            for h in range(2):
                gp[h, i] = total[:, h * LANES:(h + 1) * LANES]
            for k in range(3):
                trade(k, i).start()
        for i in range(half):
            for k in range(3):
                trade(k, i).wait_recv()
        for i in range(half):
            gfull[side * half + i] = gp[side, i] + ax[1, i]
            gfull[(1 - side) * half + i] = ax[0, i] + ax[2, i]
        for d in range(n_dp):
            for s in range(SLOTS):
                slot_out[d, s] = gfull[idx_ref[d * SLOTS + s]] * valid_ref[d * SLOTS + s]
        for o in range(1, n_dp):
            deliver(o).start()
        slot_in[side, dp] = slot_out[dp]
        for j in range(last):
            finish(j)
        for o in range(1, n_dp):
            deliver(o).wait_recv()
        share.start()
        share.wait_recv()
        scale = 1.0 / math.sqrt(tokens * n_dp)
        for s in range(SLOTS):
            whole = []
            for h in range(2):
                rows = []
                for p in range(n_dp):
                    source = 2 * (p % n_line) + lax.rem(p // n_line + group, 2)
                    rows.append(slot_in[h, source, s])
                whole.append(jnp.concatenate(rows, axis=0) * scale)
            corner, beside = whole
            upper = jnp.where(row < column, corner, 0.0)
            lower = jnp.where(row > column, corner, 0.0)
            grad_ref[s, :LANES, :LANES] = upper - upper.T
            grad_ref[s, LANES:, LANES:] = lower - lower.T
            grad_ref[s, :LANES, LANES:] = beside
            grad_ref[s, LANES:, :LANES] = -beside.T
        finish(last)
        for i in range(half):
            swap(i).wait_send()
            cross(i).wait_send()
            for o in range(1, n_line):
                along(i, o).wait_send()
            for k in range(3):
                trade(k, i).wait_send()
        for o in range(1, n_dp):
            deliver(o).wait_send()
        share.wait_send()
    else:
        for j in range(last + 1):
            finish(j)
    for i in range(half):
        tell(i).wait_send()
    for j in range(last + 1):
        for i in range(per):
            for o in range(half_mp):
                first(j, o, i).wait_send()
            for o in range(1, half_mp):
                second(j, o, i).wait_send()


def publish(first, second):
    def body(a_ref, b_ref, oa_ref, ob_ref, sems):
        one = pltpu.make_async_copy(a_ref, oa_ref, sems.at[0])
        two = pltpu.make_async_copy(b_ref, ob_ref, sems.at[1])
        one.start()
        two.start()
        one.wait()
        two.wait()

    vmem = pl.BlockSpec(memory_space=pltpu.VMEM)
    hbm = pl.BlockSpec(memory_space=pl.ANY)
    return pl.pallas_call(
        body,
        out_shape=(jax.ShapeDtypeStruct(first.shape, first.dtype), jax.ShapeDtypeStruct(second.shape, second.dtype)),
        in_specs=[vmem, vmem],
        out_specs=(hbm, hbm),
        scratch_shapes=[pltpu.SemaphoreType.DMA((2,))],
        compiler_params=pltpu.CompilerParams(vmem_limit_bytes=2 * 1024 * 1024),
    )(first, second)


def local(n_dp, n_mp, activations, cotangent, frozen_weight, skew_params, tile_order, block_owner):
    tokens, dim = activations.shape
    hidden = cotangent.shape[1]
    blocks, block, _ = skew_params.shape
    tiles = tile_order.shape[0]
    piece = block // 2 // n_dp
    own_gram = piece * n_dp * 2 == block and piece % 8 == 0 and n_dp % 2 == 0 and n_mp == 4 and block == 2 * LANES
    keep = piece if own_gram else 8
    ring = n_dp if own_gram else 2
    half = blocks // 2
    some = half if own_gram else 1
    n_line = ring // 2
    half_mp = n_mp // 2
    per = tiles // n_mp
    span = max(half_mp - 1, 1)
    sizes = [z - a for a, z in cuts(tokens)]
    count = len(sizes)

    cfg = (tokens, dim, block, blocks, tiles, n_dp, n_mp, own_gram)
    vmem = pl.BlockSpec(memory_space=pltpu.VMEM)
    dma = pltpu.SemaphoreType.DMA
    grad_shape = (SLOTS if own_gram else blocks, block, block)
    squares = pltpu.VMEM((half, block, block), F32)
    gram = pltpu.VMEM((some, block, block), F32)

    def by_chunk(*lead):
        return tuple(pltpu.VMEM((*lead, rows, LANES), F32) for rows in sizes)

    input_grad, grads = pl.pallas_call(
        functools.partial(kernel, cfg),
        out_shape=(jax.ShapeDtypeStruct((tokens, dim // n_mp), BF16), jax.ShapeDtypeStruct(grad_shape, F32)),
        in_specs=[pl.BlockSpec(memory_space=pltpu.SMEM)] + [pl.BlockSpec(memory_space=pl.ANY)] * 4,
        out_specs=(vmem, vmem),
        scratch_shapes=[
            pltpu.SMEM((tiles,), jnp.int32),
            pltpu.SMEM((n_dp * SLOTS,), jnp.int32),
            pltpu.SMEM((n_dp * SLOTS,), F32),
            pltpu.VMEM((hidden, tokens), BF16),
            pltpu.VMEM((tokens, hidden), BF16),
            pltpu.VMEM((hidden, dim), BF16),
            pltpu.VMEM((blocks, block, block), BF16),
            pltpu.VMEM((tiles, tokens, LANES), BF16),
            pltpu.VMEM((tiles, tokens, LANES), F32),
            by_chunk(tiles),
            by_chunk(half_mp, per),
            by_chunk(half_mp, per),
            by_chunk(span, per),
            by_chunk(span, per),
            pltpu.VMEM((half, block, block), BF16),
            pltpu.VMEM((half, block, block), BF16),
            pltpu.VMEM((blocks, block, block), BF16),
            pltpu.VMEM((blocks, block, block), BF16),
            squares, squares,
            gram, gram, gram,
            pltpu.VMEM((some, 2, n_line, keep, block), F32),
            pltpu.VMEM((some, n_line, keep, block), F32),
            pltpu.VMEM((some, n_line, keep, block), F32),
            pltpu.VMEM((some, max(n_line - 1, 1), keep, block), F32),
            pltpu.VMEM((2, some, keep, LANES), F32),
            pltpu.VMEM((3, some, keep, LANES), F32),
            pltpu.VMEM((2 * some, keep, LANES), F32),
            pltpu.VMEM((ring, SLOTS, keep, LANES), F32),
            pltpu.VMEM((2, ring, SLOTS, keep, LANES), F32),
            dma((blocks,)), dma((tiles,)), dma((2,)),
            dma((half,)), dma((half,)),
            dma((count, half_mp, per)), dma((count, half_mp, per)),
            dma((count, span, per)), dma((count, span, per)),
            dma((half,)), dma((half,)),
            dma((half,)), dma((half,)),
            dma((half, max(n_line - 1, 1))), dma((half, max(n_line - 1, 1))),
            dma((3, half)), dma((3, half)),
            dma((ring,)), dma((ring,)),
            dma((1,)), dma((1,)),
        ],
        compiler_params=pltpu.CompilerParams(
            collective_id=0, has_side_effects=True, vmem_limit_bytes=52 * 1024 * 1024),
    )(jnp.concatenate([tile_order, block_owner]), activations, cotangent.T, frozen_weight.T, skew_params)
    if own_gram:
        return publish(input_grad, grads)
    numbers = jnp.arange(blocks, dtype=jnp.int32)
    same = block_owner[:, None] == block_owner[None, :]
    rank = jnp.sum((same & (numbers[:, None] > numbers[None, :])).astype(jnp.int32), axis=1)
    place = block_owner * SLOTS + rank
    chosen = place[None, :] == jnp.arange(n_dp * SLOTS, dtype=jnp.int32)[:, None]
    index = jnp.sum(jnp.where(chosen, numbers[None, :], 0), axis=1)
    valid = jnp.sum(chosen.astype(F32), axis=1)
    gram = lax.psum(grads, ("dp", "mp"))
    at = lax.axis_index("dp") * SLOTS
    mine = lax.dynamic_slice(index, (at,), (SLOTS,))
    used = lax.dynamic_slice(valid, (at,), (SLOTS,))
    g = jnp.take(gram, mine, axis=0) * used[:, None, None]
    plain = jnp.take(skew_params, mine, axis=0).astype(F32)
    qt = jnp.swapaxes(plain, 1, 2) - plain
    mul = functools.partial(jnp.einsum, "bij,bjk->bik", precision=lax.Precision.HIGHEST)
    left = mul(g, qt)
    both = left + mul(qt, g)
    total = 2.0 * g + 2.0 * both + mul(left, qt) + mul(qt, both)
    return input_grad, (total - jnp.swapaxes(total, 1, 2)) * (1.0 / math.sqrt(tokens * n_dp))


def solution(mesh):
    placed = (P("dp", None), P("dp", "mp"), P(None, "mp"), P(), P(), P())
    return jax.shard_map(
        functools.partial(local, mesh.shape["dp"], mesh.shape["mp"]),
        mesh=mesh,
        in_specs=placed,
        out_specs=(P("dp", "mp"), P("dp", None, None)),
        check_vma=False,
    )
```

```python
import functools
import math

import jax
import jax.numpy as jnp
from jax import lax
from jax.experimental import pallas as pl
from jax.experimental.pallas import tpu as pltpu
from jax.sharding import PartitionSpec as P

SLOTS = 3
AHEAD = 4
LANES = 128
MESH = pl.DeviceIdType.MESH
F32 = jnp.float32
BF16 = jnp.bfloat16

NN = (((1,), (0,)), ((), ()))
TN = (((0,), (0,)), ((), ()))


def dot(a, b, dims=NN):
    return lax.dot_general(a, b, dims, preferred_element_type=F32)


def split(x):
    high = x.astype(BF16)
    return high, (x - high.astype(F32)).astype(BF16)


def dot_split(a, b):
    return dot(a[0], b[0]) + (dot(a[0], b[1]) + dot(a[1], b[0]))


def skew_of(params):
    plain = params.astype(F32)
    return plain - plain.T


def cuts(tokens):
    first = tokens * 3 // 8 // 16 * 16
    return ((0, first), (first, tokens)) if first else ((0, tokens),)


def kernel(cfg, index_ref, act_hbm, cot_hbm, w_hbm, s_hbm, out_ref, grad_ref, *scratch):
    tokens, dim, block, blocks, tiles, n_dp, n_mp, own_gram = cfg
    (inv_ref, idx_ref, valid_ref, cot_ref, cots, w_ref, s_ref, acts, feat, outblk, part, recv1, send2, recv2,
     sh, sl, eth, etl, esend, erecv, gsend, gown, grecv, pk, arecv, hsum, zrecv, gp, ax, gfull, slot_out, slot_in,
     lw, la, lo, es, er, s1, r1, s2, r2, gs, gr, xs, xr, ds, dr, ys, yr, ss, sr, ms, mr) = scratch
    half_mp = n_mp // 2
    half = blocks // 2
    per = tiles // n_mp
    chunks = cuts(tokens)
    last = len(chunks) - 1
    dp = lax.axis_index("dp")
    mp = lax.axis_index("mp")
    side = lax.rem(mp, 2)
    group = mp // 2
    mate = group * 2 + (1 - side)

    load_s = pltpu.make_async_copy(s_hbm, s_ref, lo.at[0])
    load_cot = pltpu.make_async_copy(cot_hbm, cot_ref, lo.at[1])

    def load_w(n):
        at = pl.ds(pl.multiple_of(n * block, block), block)
        return pltpu.make_async_copy(w_hbm.at[:, at], w_ref.at[:, at], lw.at[n])

    def load_act(k):
        return pltpu.make_async_copy(act_hbm.at[:, k * LANES:(k + 1) * LANES], acts.at[k], la.at[k])

    load_s.start()
    load_cot.start()
    for n in range(AHEAD):
        load_w(n).start()

    def same_side(offset):
        return lax.rem(group + offset, half_mp)

    barrier = pltpu.get_barrier_semaphore()
    peers = []
    for o in range(half_mp):
        for k in range(2):
            if o or k:
                peers.append((dp, same_side(o) * 2 + (side if k == 0 else 1 - side)))
    if own_gram:
        for o in range(1, n_dp):
            peers.append((lax.rem(dp + o, n_dp), mp))
        for k in range(2):
            peers.append((dp + 1 - 2 * lax.rem(dp, 2), (1 - group) * 2 + (side if k == 0 else 1 - side)))
    for peer in peers:
        pl.semaphore_signal(barrier, inc=1, device_id=peer, device_id_type=MESH)

    def invert(k, _):
        found = jnp.int32(0)
        for i in range(tiles):
            found = jnp.where(index_ref[i] == k, i, found)
        inv_ref[k] = found
        return 0


    lax.fori_loop(0, tiles, invert, 0)

    def tell(i):
        return pltpu.make_async_remote_copy(
            src_ref=esend.at[i], dst_ref=erecv.at[i], send_sem=es.at[i], recv_sem=er.at[i],
            device_id=(dp, mate), device_id_type=MESH)

    load_s.wait()
    for i in range(half):
        b = side * half + i
        skew = skew_of(s_ref[b])
        pair = split(skew)
        sh[i], sl[i] = pair
        square = dot_split(pair, pair)
        cube = dot_split(split(square), pair)
        turned = 2.0 * square - 2.0 * skew - cube
        esend[i] = turned
        eth[b], etl[b] = split(turned)
    pl.semaphore_wait(barrier, len(peers))
    for i in range(half):
        tell(i).start()
    for n in range(AHEAD, blocks):
        load_w(n).start()

    load_cot.wait()
    for i in range(tokens // LANES):
        cots[i * LANES:(i + 1) * LANES, :] = cot_ref[:, i * LANES:(i + 1) * LANES].T

    def feature(n, at):
        a, z = at
        f = dot(cots[a:z, :], w_ref[:, pl.ds(pl.multiple_of(n * block, block), block)])
        feat[2 * n, a:z] = f[:, :LANES]
        feat[2 * n + 1, a:z] = f[:, LANES:]

    def first_features(k, _):
        for u in range(2):
            load_w(2 * k + u).wait()
        for u in range(2):
            feature(2 * k + u, chunks[0])
        return 0

    def rotate(j):
        a, z = chunks[j]

        def body(k, _):
            for u in range(half):
                b = k * half + u
                f = jnp.concatenate([feat[index_ref[2 * b], a:z], feat[index_ref[2 * b + 1], a:z]], axis=1)
                high, low = split(f)
                out = f + (dot(high, eth[b]) + (dot(low, eth[b]) + dot(high, etl[b])))
                outblk[j][2 * b] = out[:, :LANES]
                outblk[j][2 * b + 1] = out[:, LANES:]
            return 0
        lax.fori_loop(0, 2, body, 0)

    def first(j, o, i):
        q = same_side(o)
        return pltpu.make_async_remote_copy(
            src_ref=part[j].at[q, i], dst_ref=recv1[j].at[q, i],
            send_sem=s1.at[j, o, i], recv_sem=r1.at[j, o, i],
            device_id=(dp, mate), device_id_type=MESH)

    def second(j, o, i):
        return pltpu.make_async_remote_copy(
            src_ref=send2[j].at[o - 1, i], dst_ref=recv2[j].at[o - 1, i],
            send_sem=s2.at[j, o - 1, i], recv_sem=r2.at[j, o - 1, i],
            device_id=(dp, same_side(o) * 2 + side), device_id_type=MESH)

    def start_first(j):
        for o in list(range(1, half_mp)) + [0]:
            q = same_side(o)
            for i in range(per):
                part[j][q, i] = outblk[j][inv_ref[(q * 2 + (1 - side)) * per + i]]
                first(j, o, i).start()

    def start_second(j):
        for o in range(1, half_mp):
            q = same_side(o)
            for i in range(per):
                first(j, o, i).wait_recv()
                send2[j][o - 1, i] = outblk[j][inv_ref[(q * 2 + side) * per + i]] + recv1[j][q, i]
                second(j, o, i).start()

    def finish(j):
        a, z = chunks[j]
        for i in range(per):
            first(j, 0, i).wait_recv()
            total = outblk[j][inv_ref[mp * per + i]] + recv1[j][group, i]
            for o in range(1, half_mp):
                second(j, o, i).wait_recv()
                total = total + recv2[j][o - 1, i]
            out_ref[a:z, i * LANES:(i + 1) * LANES] = total.astype(out_ref.dtype)

    def gram_of(b):
        t0 = index_ref[2 * b]
        t1 = index_ref[2 * b + 1]
        high, low = split(jnp.concatenate([feat[t0], feat[t1]], axis=1))
        x = jnp.concatenate([acts[t0], acts[t1]], axis=1)
        return dot(x, high, TN) + dot(x, low, TN)

    def swap(i):
        return pltpu.make_async_remote_copy(
            src_ref=gsend.at[i], dst_ref=grecv.at[i], send_sem=gs.at[i], recv_sem=gr.at[i],
            device_id=(dp, mate), device_id_type=MESH)

    lax.fori_loop(0, blocks // 2, first_features, 0)
    for i in range(half):
        tell(i).wait_recv()
        b = (1 - side) * half + i
        eth[b], etl[b] = split(erecv[i])
    rotate(0)
    start_first(0)
    for k in range(tiles):
        load_act(k).start()
    for j in range(1, last + 1):
        for n in range(half):
            feature(n, chunks[j])
        start_second(j - 1)
        for n in range(half, blocks):
            feature(n, chunks[j])
    for k in range(tiles):
        load_act(k).wait()

    if own_gram:
        parity = lax.rem(dp, 2)
        line = dp // 2
        n_line = n_dp // 2
        piece = block // 2 // n_dp
        mine = lax.rem(parity + group, 2)
        across = dp + 1 - 2 * parity

        def cross(i):
            return pltpu.make_async_remote_copy(
                src_ref=pk.at[i, 1 - mine], dst_ref=arecv.at[i], send_sem=xs.at[i], recv_sem=xr.at[i],
                device_id=(across, mp), device_id_type=MESH)

        def along(i, o):
            to = lax.rem(line + o, n_line)
            return pltpu.make_async_remote_copy(
                src_ref=hsum.at[i, to], dst_ref=zrecv.at[i, o - 1],
                send_sem=ds.at[i, o - 1], recv_sem=dr.at[i, o - 1],
                device_id=(to * 2 + parity, mp), device_id_type=MESH)

        def trade(k, i):
            column = side if k == 1 else 1 - side
            to = (dp, mate) if k == 0 else (across, (1 - group) * 2 + column)
            return pltpu.make_async_remote_copy(
                src_ref=gp.at[column, i], dst_ref=ax.at[k, i], send_sem=ys.at[k, i], recv_sem=yr.at[k, i],
                device_id=to, device_id_type=MESH)

        def deliver(o):
            to = lax.rem(dp + o, n_dp)
            return pltpu.make_async_remote_copy(
                src_ref=slot_out.at[to], dst_ref=slot_in.at[side, dp],
                send_sem=ss.at[o], recv_sem=sr.at[o],
                device_id=(to, mp), device_id_type=MESH)

        share = pltpu.make_async_remote_copy(
            src_ref=slot_in.at[side], dst_ref=slot_in.at[side], send_sem=ms.at[0], recv_sem=mr.at[0],
            device_id=(dp, mate), device_id_type=MESH)

        row = lax.broadcasted_iota(jnp.int32, (LANES, LANES), 0)
        column = lax.broadcasted_iota(jnp.int32, (LANES, LANES), 1)

        for i in range(half):
            gsend[i] = gram_of((1 - side) * half + i)
            swap(i).start()
        for i in range(half):
            gown[i] = gram_of(side * half + i)
        for i in range(half):
            swap(i).wait_recv()
        for i in range(half):
            g = gown[i] + grecv[i]
            turned = g.T
            odd = g - turned
            pair = (sh[i], sl[i])
            once = dot_split(split(odd), pair)
            twice = dot_split(split(2.0 * (g + turned) - once - 0.5 * once.T), pair)
            x = odd - twice
            upper = x[:LANES, :LANES]
            lower = x[LANES:, LANES:]
            corner = jnp.where(row < column, upper - upper.T, lower - lower.T)
            packed = jnp.concatenate([corner, x[:LANES, LANES:] - x[LANES:, :LANES].T], axis=1)
            for h in range(2):
                for q in range(n_line):
                    at = (h * n_line + q) * piece
                    pk[i, h, q] = packed[at:at + piece]
        for i in range(half):
            cross(i).start()
    else:
        for b in range(blocks):
            grad_ref[b] = gram_of(b)

    if last:
        rotate(last)
        start_first(last)
    start_second(last)

    if own_gram:
        for i in range(half):
            cross(i).wait_recv()
            hsum[i] = pk[i, mine] + arecv[i]
            for o in range(1, n_line):
                along(i, o).start()

        places = []
        for b in range(blocks):
            place = index_ref[tiles + b] * SLOTS
            for e in range(b):
                place = place + jnp.where(index_ref[tiles + e] == index_ref[tiles + b], 1, 0)
            places.append(place)

        def locate(q, _):
            found = jnp.int32(0)
            count = jnp.float32(0.0)
            for b in range(blocks):
                found = jnp.where(places[b] == q, b, found)
                count = jnp.where(places[b] == q, 1.0, count)
            idx_ref[q] = found
            valid_ref[q] = count
            return 0

        lax.fori_loop(0, n_dp * SLOTS, locate, 0)

        for i in range(half):
            total = hsum[i, line]
            for o in range(1, n_line):
                along(i, o).wait_recv()
                total = total + zrecv[i, o - 1]
            for h in range(2):
                gp[h, i] = total[:, h * LANES:(h + 1) * LANES]
            for k in range(3):
                trade(k, i).start()
        for i in range(half):
            for k in range(3):
                trade(k, i).wait_recv()
        for i in range(half):
            gfull[side * half + i] = gp[side, i] + ax[1, i]
            gfull[(1 - side) * half + i] = ax[0, i] + ax[2, i]
        for d in range(n_dp):
            for s in range(SLOTS):
                slot_out[d, s] = gfull[idx_ref[d * SLOTS + s]] * valid_ref[d * SLOTS + s]
        for o in range(1, n_dp):
            deliver(o).start()
        slot_in[side, dp] = slot_out[dp]
        for j in range(last):
            finish(j)
        for o in range(1, n_dp):
            deliver(o).wait_recv()
        share.start()
        finish(last)
        share.wait_recv()
        scale = 1.0 / math.sqrt(tokens * n_dp)
        for s in range(SLOTS):
            whole = []
            for h in range(2):
                rows = []
                for p in range(n_dp):
                    source = 2 * (p % n_line) + lax.rem(p // n_line + group, 2)
                    rows.append(slot_in[h, source, s])
                whole.append(jnp.concatenate(rows, axis=0) * scale)
            corner, beside = whole
            upper = jnp.where(row < column, corner, 0.0)
            lower = jnp.where(row > column, corner, 0.0)
            grad_ref[s, :LANES, :LANES] = upper - upper.T
            grad_ref[s, LANES:, LANES:] = lower - lower.T
            grad_ref[s, :LANES, LANES:] = beside
            grad_ref[s, LANES:, :LANES] = -beside.T
        for i in range(half):
            swap(i).wait_send()
            cross(i).wait_send()
            for o in range(1, n_line):
                along(i, o).wait_send()
            for k in range(3):
                trade(k, i).wait_send()
        for o in range(1, n_dp):
            deliver(o).wait_send()
        share.wait_send()
    else:
        for j in range(last + 1):
            finish(j)
    for i in range(half):
        tell(i).wait_send()
    for j in range(last + 1):
        for i in range(per):
            for o in range(half_mp):
                first(j, o, i).wait_send()
            for o in range(1, half_mp):
                second(j, o, i).wait_send()


def publish(first, second):
    def body(a_ref, b_ref, oa_ref, ob_ref, sems):
        one = pltpu.make_async_copy(a_ref, oa_ref, sems.at[0])
        two = pltpu.make_async_copy(b_ref, ob_ref, sems.at[1])
        one.start()
        two.start()
        one.wait()
        two.wait()

    vmem = pl.BlockSpec(memory_space=pltpu.VMEM)
    hbm = pl.BlockSpec(memory_space=pl.ANY)
    return pl.pallas_call(
        body,
        out_shape=(jax.ShapeDtypeStruct(first.shape, first.dtype), jax.ShapeDtypeStruct(second.shape, second.dtype)),
        in_specs=[vmem, vmem],
        out_specs=(hbm, hbm),
        scratch_shapes=[pltpu.SemaphoreType.DMA((2,))],
        compiler_params=pltpu.CompilerParams(vmem_limit_bytes=2 * 1024 * 1024),
    )(first, second)


def local(n_dp, n_mp, activations, cotangent, frozen_weight, skew_params, tile_order, block_owner):
    tokens, dim = activations.shape
    hidden = cotangent.shape[1]
    blocks, block, _ = skew_params.shape
    tiles = tile_order.shape[0]
    piece = block // 2 // n_dp
    own_gram = piece * n_dp * 2 == block and piece % 8 == 0 and n_dp % 2 == 0 and n_mp == 4 and block == 2 * LANES
    keep = piece if own_gram else 8
    ring = n_dp if own_gram else 2
    half = blocks // 2
    some = half if own_gram else 1
    n_line = ring // 2
    half_mp = n_mp // 2
    per = tiles // n_mp
    span = max(half_mp - 1, 1)
    sizes = [z - a for a, z in cuts(tokens)]
    count = len(sizes)

    cfg = (tokens, dim, block, blocks, tiles, n_dp, n_mp, own_gram)
    vmem = pl.BlockSpec(memory_space=pltpu.VMEM)
    dma = pltpu.SemaphoreType.DMA
    grad_shape = (SLOTS if own_gram else blocks, block, block)
    squares = pltpu.VMEM((half, block, block), F32)
    gram = pltpu.VMEM((some, block, block), F32)

    def by_chunk(*lead):
        return tuple(pltpu.VMEM((*lead, rows, LANES), F32) for rows in sizes)

    input_grad, grads = pl.pallas_call(
        functools.partial(kernel, cfg),
        out_shape=(jax.ShapeDtypeStruct((tokens, dim // n_mp), BF16), jax.ShapeDtypeStruct(grad_shape, F32)),
        in_specs=[pl.BlockSpec(memory_space=pltpu.SMEM)] + [pl.BlockSpec(memory_space=pl.ANY)] * 4,
        out_specs=(vmem, vmem),
        scratch_shapes=[
            pltpu.SMEM((tiles,), jnp.int32),
            pltpu.SMEM((n_dp * SLOTS,), jnp.int32),
            pltpu.SMEM((n_dp * SLOTS,), F32),
            pltpu.VMEM((hidden, tokens), BF16),
            pltpu.VMEM((tokens, hidden), BF16),
            pltpu.VMEM((hidden, dim), BF16),
            pltpu.VMEM((blocks, block, block), BF16),
            pltpu.VMEM((tiles, tokens, LANES), BF16),
            pltpu.VMEM((tiles, tokens, LANES), F32),
            by_chunk(tiles),
            by_chunk(half_mp, per),
            by_chunk(half_mp, per),
            by_chunk(span, per),
            by_chunk(span, per),
            pltpu.VMEM((half, block, block), BF16),
            pltpu.VMEM((half, block, block), BF16),
            pltpu.VMEM((blocks, block, block), BF16),
            pltpu.VMEM((blocks, block, block), BF16),
            squares, squares,
            gram, gram, gram,
            pltpu.VMEM((some, 2, n_line, keep, block), F32),
            pltpu.VMEM((some, n_line, keep, block), F32),
            pltpu.VMEM((some, n_line, keep, block), F32),
            pltpu.VMEM((some, max(n_line - 1, 1), keep, block), F32),
            pltpu.VMEM((2, some, keep, LANES), F32),
            pltpu.VMEM((3, some, keep, LANES), F32),
            pltpu.VMEM((2 * some, keep, LANES), F32),
            pltpu.VMEM((ring, SLOTS, keep, LANES), F32),
            pltpu.VMEM((2, ring, SLOTS, keep, LANES), F32),
            dma((blocks,)), dma((tiles,)), dma((2,)),
            dma((half,)), dma((half,)),
            dma((count, half_mp, per)), dma((count, half_mp, per)),
            dma((count, span, per)), dma((count, span, per)),
            dma((half,)), dma((half,)),
            dma((half,)), dma((half,)),
            dma((half, max(n_line - 1, 1))), dma((half, max(n_line - 1, 1))),
            dma((3, half)), dma((3, half)),
            dma((ring,)), dma((ring,)),
            dma((1,)), dma((1,)),
        ],
        compiler_params=pltpu.CompilerParams(
            collective_id=0, has_side_effects=True, vmem_limit_bytes=52 * 1024 * 1024),
    )(jnp.concatenate([tile_order, block_owner]), activations, cotangent.T, frozen_weight.T, skew_params)
    if own_gram:
        return publish(input_grad, grads)
    numbers = jnp.arange(blocks, dtype=jnp.int32)
    same = block_owner[:, None] == block_owner[None, :]
    rank = jnp.sum((same & (numbers[:, None] > numbers[None, :])).astype(jnp.int32), axis=1)
    place = block_owner * SLOTS + rank
    chosen = place[None, :] == jnp.arange(n_dp * SLOTS, dtype=jnp.int32)[:, None]
    index = jnp.sum(jnp.where(chosen, numbers[None, :], 0), axis=1)
    valid = jnp.sum(chosen.astype(F32), axis=1)
    gram = lax.psum(grads, ("dp", "mp"))
    at = lax.axis_index("dp") * SLOTS
    mine = lax.dynamic_slice(index, (at,), (SLOTS,))
    used = lax.dynamic_slice(valid, (at,), (SLOTS,))
    g = jnp.take(gram, mine, axis=0) * used[:, None, None]
    plain = jnp.take(skew_params, mine, axis=0).astype(F32)
    qt = jnp.swapaxes(plain, 1, 2) - plain
    mul = functools.partial(jnp.einsum, "bij,bjk->bik", precision=lax.Precision.HIGHEST)
    left = mul(g, qt)
    both = left + mul(qt, g)
    total = 2.0 * g + 2.0 * both + mul(left, qt) + mul(qt, both)
    return input_grad, (total - jnp.swapaxes(total, 1, 2)) * (1.0 / math.sqrt(tokens * n_dp))


def solution(mesh):
    placed = (P("dp", None), P("dp", "mp"), P(None, "mp"), P(), P(), P())
    return jax.shard_map(
        functools.partial(local, mesh.shape["dp"], mesh.shape["mp"]),
        mesh=mesh,
        in_specs=placed,
        out_specs=(P("dp", "mp"), P("dp", None, None)),
        check_vma=False,
    )
```
